32 devices in a mesh: aa: 4 (over z), ba: 8 (over y, x, core).
Axes of the slice: x: 2, y: 2, z: 4, core: 2. Of those that a mesh axis runs over, the one named last changes fastest.
Arguments:
- atom_cond: float32 [12288, 128], P(('aa', 'ba')), may hold values from -6 to 6
- noisy_pos: float32 [3, 12288], P(None, ('aa', 'ba')), may hold values from -8 to 8
- noise_level: float32 [1], replicated, may hold values from 0.1 to 4
- atom_token: int32 [12288], P(('aa', 'ba')), may hold values from -1 to 1023, as said below
- token_cond: float32 [1024, 768], P('aa'), may hold values from -6 to 6
- pair: bfloat16 [1024, 1024, 128], P('aa', 'ba'), may hold values from -64 to 64
- pair_bias_weight: bfloat16 [16, 128], replicated, may hold values from -0.375 to 0.375
- gains: float32 [3, 768], replicated, may hold values from 0.25 to 1.75
- w_pos: float32 [3, 128], replicated, may hold values from -3.5 to 3.5
- w_atom_token: bfloat16 [128, 768], replicated, may hold values from -0.5 to 0.5
- w_query_gate: bfloat16 [768, 1536], replicated, may hold values from -0.21875 to 0.21875
- w_key_value: bfloat16 [768, 1536], replicated, may hold values from -0.21875 to 0.21875
- w_attn_out: bfloat16 [768, 768], replicated, may hold values from -0.21875 to 0.21875
- w_up: bfloat16 [768, 3072], replicated, may hold values from -0.21875 to 0.21875
- w_down: bfloat16 [1536, 768], replicated, may hold values from -0.15625 to 0.15625
- w_token_atom: bfloat16 [768, 128], replicated, may hold values from -0.21875 to 0.21875
- w_pos_out: bfloat16 [3, 128], replicated, may hold values from -0.5 to 0.5
Outputs:
- denoised: float32 [3, 12288], P(None, ('aa', 'ba'))
- token_out: float32 [1024, 768], P('aa')
The draws below stay inside these ranges and needn't reach their ends.
Inputs may be any that keep to these rules, and one draw needn't show every extreme that they name: `atom_token`: atom slots come in 4 groups of 3072 consecutive slots; group r holds only atoms of tokens r * 256 to (r + 1) * 256 - 1, in nondecreasing token order, live slots first and -1 after them. Every token has 1 to 12 atoms, and some token of every group has exactly 12.
All inputs are finite; a program needn't handle non-finite values.
Results may differ from the reference program's by a relative error of at most 0.01.
Values may be sent and summed in bfloat16 or wider, within the bound.
A program may use at most 128 MiB of HBM per device.

```python
import math
import jax
import jax.numpy as jnp
from jax import lax

D = 768
HEADS = 16
PAIR_C = 128
ATOM_C = 128
FF = 1536
TOK_A = 256
PER_TOKEN = 12
TOKENS = 1024
ATOMS = 12288
N_BA = 8


def bias_table(key):
    return 0.125 * jax.random.truncated_normal(jax.random.fold_in(key, 11), -3.0, 3.0, (HEADS, PAIR_C), jnp.float32)


def draw_pair_bias_weight(key, part):
    return bias_table(key).astype(jnp.bfloat16)


def draw_pair(key, part):
    base_key = jax.random.fold_in(key, 12)
    field = jax.random.truncated_normal(base_key, -6.0, 6.0, (TOKENS, TOKENS, PAIR_C), jnp.float32)
    table = bias_table(key).astype(jnp.bfloat16).astype(jnp.float32)
    pick_rows = jax.random.randint(jax.random.fold_in(key, 13), (HEADS, 3), 0, TOKENS)
    pick_cols = jax.random.randint(jax.random.fold_in(key, 14), (HEADS, 3), 0, TOKENS)
    pick_steps = jax.random.randint(jax.random.fold_in(key, 15), (HEADS, 3), 1, TOKENS)
    for head_index in range(HEADS):
        sign_row = jnp.sign(table[head_index])
        weight_total = jnp.maximum(jnp.sum(jnp.abs(table[head_index])), 0.5)
        for level_index, strength in enumerate((120.0, 180.0, 240.0)):
            row_pick = pick_rows[head_index, level_index]
            first_col = pick_cols[head_index, level_index]
            second_col = (first_col + pick_steps[head_index, level_index]) % TOKENS
            field = field.at[row_pick, first_col].set(strength / weight_total * sign_row)
            field = field.at[row_pick, second_col].set((strength - 2.0) / weight_total * sign_row)
    return field.astype(jnp.bfloat16)


def draw_atom_token(key, part):
    groups = TOKENS // TOK_A
    upper_count = jax.random.randint(jax.random.fold_in(key, 21), (groups, 1), PER_TOKEN // 2, PER_TOKEN + 1)
    raw_bits = jax.random.randint(jax.random.fold_in(key, 22), (groups, TOK_A), 0, 1 << 20)
    counts = 1 + raw_bits % upper_count
    chosen = jax.random.randint(jax.random.fold_in(key, 23), (groups, 1), 0, TOK_A)
    counts = jnp.where(jnp.arange(TOK_A, dtype=jnp.int32)[None, :] == chosen, PER_TOKEN, counts)
    ends = jnp.cumsum(counts, axis=1)
    slots = jnp.arange(PER_TOKEN * TOK_A, dtype=jnp.int32)
    owner = jnp.sum((ends[:, None, :] <= slots[None, :, None]).astype(jnp.int32), axis=2)
    token_ids = owner + (jnp.arange(groups, dtype=jnp.int32) * TOK_A)[:, None]
    return jnp.where(owner < TOK_A, token_ids, -1).reshape(-1).astype(jnp.int32)


def level_of(stream_key, dims, cuts, low, high):
    factor_of = 1.0
    for dim, parts in cuts:
        draws = jax.random.uniform(jax.random.fold_in(jax.random.fold_in(stream_key, 6), dim), (parts,), jnp.float32, low / len(cuts), high / len(cuts))
        factor_of = factor_of * jnp.repeat(jnp.exp(draws), dims[dim] // parts).reshape((-1,) + (1,) * (len(dims) - 1 - dim))
    return factor_of


def centred(stream_key, shape, width, reach, shards=(), held_as=jnp.bfloat16):
    factor_of = level_of(stream_key, shape, shards, -0.22, 0.18) if shards else 1.0
    entries = jax.random.normal(stream_key, shape, jnp.float32) * width * factor_of
    return jnp.minimum(jnp.maximum(entries, -reach), reach).astype(held_as)


def setup_inputs(seed: int = 0) -> dict:
    streams_of = jax.random.split(jax.random.key(seed), 18)
    return {
        "atom_cond": centred(streams_of[0], (ATOMS, ATOM_C), 1.0, 6.0, ((0, 32),), jnp.float32),
        "noisy_pos": centred(streams_of[1], (3, ATOMS), 1.5, 8.0, ((1, 32),), jnp.float32),
        "noise_level": jnp.clip(jnp.exp(jax.random.uniform(streams_of[2], (1,), jnp.float32, math.log(0.1), math.log(4.0))), 0.1, 4.0),
        "atom_token": draw_atom_token(jax.random.fold_in(streams_of[17], 71), 0),
        "token_cond": centred(streams_of[4], (TOKENS, D), 1.0, 6.0, ((0, 4),), jnp.float32),
        "pair": draw_pair(jax.random.fold_in(streams_of[17], 71), 0),
        "pair_bias_weight": draw_pair_bias_weight(jax.random.fold_in(streams_of[17], 71), 0),
        "gains": jnp.clip(1.0 + 0.15 * jax.random.normal(streams_of[7], (3, D), jnp.float32), 0.25, 1.75),
        "w_pos": centred(streams_of[8], (3, ATOM_C), 3 ** -0.5, 3.5, (), jnp.float32),
        "w_atom_token": centred(streams_of[9], (ATOM_C, D), ATOM_C ** -0.5, 0.5),
        "w_query_gate": centred(streams_of[10], (D, 2 * D), D ** -0.5, 0.21875),
        "w_key_value": centred(streams_of[11], (D, 2 * D), D ** -0.5, 0.21875),
        "w_attn_out": centred(streams_of[12], (D, D), D ** -0.5, 0.21875),
        "w_up": centred(streams_of[13], (D, 2 * FF), D ** -0.5, 0.21875),
        "w_down": centred(streams_of[14], (FF, D), FF ** -0.5, 0.15625),
        "w_token_atom": centred(streams_of[15], (D, ATOM_C), D ** -0.5, 0.21875),
        "w_pos_out": centred(streams_of[16], (3, ATOM_C), ATOM_C ** -0.5, 0.5),
    }


def layer_norm(values, gain_row):
    mean_value = lax.optimization_barrier(jnp.mean(values, axis=-1, keepdims=True))
    centered = values - mean_value
    variance = lax.optimization_barrier(jnp.mean(centered * centered, axis=-1, keepdims=True))
    return centered * lax.rsqrt(variance + 1e-05) * gain_row

def reference(atom_cond, noisy_pos, noise_level, atom_token, token_cond, pair, pair_bias_weight, gains, w_pos, w_atom_token, w_query_gate, w_key_value, w_attn_out, w_up, w_down, w_token_atom, w_pos_out):
    noise_sigma = noise_level[0]
    inv_scale = 1.0 / jnp.sqrt(noise_sigma * noise_sigma + 1.0)
    scaled_pos = noisy_pos * inv_scale
    atom_state = atom_cond + scaled_pos[0][:, None] * w_pos[0]
    atom_state = atom_state + scaled_pos[1][:, None] * w_pos[1]
    atom_state = atom_state + scaled_pos[2][:, None] * w_pos[2]
    hidden_atom = jax.nn.relu(jnp.dot(atom_state.astype(jnp.bfloat16), w_atom_token, preferred_element_type=jnp.float32)).astype(jnp.bfloat16)
    live_mask = atom_token >= 0
    segment_ids = jnp.where(live_mask, atom_token, TOKENS).astype(jnp.int32)
    summed = jax.ops.segment_sum(hidden_atom.astype(jnp.float32), segment_ids, num_segments=TOKENS + 1)[:TOKENS]
    counts = jax.ops.segment_sum(live_mask.astype(jnp.float32), segment_ids, num_segments=TOKENS + 1)[:TOKENS]
    tokens_start = token_cond + summed / counts[:, None]
    normed = layer_norm(tokens_start, gains[0]).astype(jnp.bfloat16)
    query_gate = jnp.dot(normed, w_query_gate, preferred_element_type=jnp.float32)
    query_rows = query_gate[:, :D].astype(jnp.bfloat16)
    gate_value = jax.nn.sigmoid(query_gate[:, D:]).astype(jnp.bfloat16)
    key_value = jnp.dot(normed, w_key_value, preferred_element_type=jnp.float32).astype(jnp.bfloat16)
    head_dim = D // HEADS
    block_cols = TOKENS // N_BA
    query_heads = query_rows.astype(jnp.float32).reshape(TOKENS, HEADS, head_dim)
    bias_weight = pair_bias_weight.astype(jnp.float32)

    def one_block(block_index):
        start_row = block_index * block_cols
        kv_block = lax.dynamic_slice_in_dim(key_value, start_row, block_cols, 0).astype(jnp.float32)
        key_heads = kv_block[:, :D].reshape(block_cols, HEADS, head_dim)
        value_heads = kv_block[:, D:].reshape(block_cols, HEADS, head_dim)
        pair_block = lax.dynamic_slice_in_dim(pair, start_row, block_cols, 1).astype(jnp.float32)
        scores = jnp.einsum('ihd,jhd->hij', query_heads, key_heads) * head_dim ** (-0.5) + jnp.einsum('hc,ijc->hij', bias_weight, pair_block)
        block_max = lax.optimization_barrier(jnp.max(scores, axis=2))
        weights = jnp.exp(scores - block_max[:, :, None])
        block_total = lax.optimization_barrier(jnp.sum(weights, axis=2))
        rounded = lax.optimization_barrier(weights.astype(jnp.bfloat16)).astype(jnp.float32)
        partial_out = jnp.einsum('hij,jhd->ihd', rounded, value_heads).reshape(TOKENS, D)
        return (block_max, block_total, partial_out)
    maxima, totals, outputs = lax.map(one_block, jnp.arange(N_BA, dtype=jnp.int32))
    overall = lax.optimization_barrier(jnp.max(maxima, axis=0))
    factors = jnp.exp(maxima - overall[None])
    total_all = lax.optimization_barrier(jnp.sum(factors * totals, axis=0))
    widened = jnp.repeat(jnp.transpose(factors, (0, 2, 1)), head_dim, axis=2)
    out_all = lax.optimization_barrier(jnp.sum(widened * outputs, axis=0))
    attended = out_all / jnp.repeat(total_all.T, head_dim, axis=1)
    mixed_heads = (attended * gate_value.astype(jnp.float32)).astype(jnp.bfloat16)
    tokens_mid = tokens_start + jnp.dot(mixed_heads, w_attn_out, preferred_element_type=jnp.float32)
    normed_mid = layer_norm(tokens_mid, gains[1]).astype(jnp.bfloat16)
    gate_up = jnp.dot(normed_mid, w_up, preferred_element_type=jnp.float32)
    inner_units = (jax.nn.silu(gate_up[:, :FF]) * gate_up[:, FF:]).astype(jnp.bfloat16)
    token_out = tokens_mid + jnp.dot(inner_units, w_down, preferred_element_type=jnp.float32)
    normed_out = layer_norm(token_out, gains[2]).astype(jnp.bfloat16)
    token_atom = jnp.dot(normed_out, w_token_atom, preferred_element_type=jnp.float32).astype(jnp.bfloat16)
    safe_ids = jnp.clip(atom_token, 0, TOKENS - 1).astype(jnp.int32)
    picked = jnp.where(live_mask[:, None], token_atom[safe_ids].astype(jnp.float32), 0.0)
    atom_final = atom_state + picked
    atom_normed = layer_norm(atom_final, 1.0).astype(jnp.bfloat16)
    update = lax.dot_general(w_pos_out, atom_normed, (((1,), (1,)), ((), ())), preferred_element_type=jnp.float32)
    denoised = noisy_pos * (inv_scale * inv_scale) + update * (noise_sigma * inv_scale)
    return (denoised, token_out)
```

```python
import functools

import jax
import jax.numpy as jnp
from jax import lax
from jax.experimental import pallas as pl
from jax.experimental.pallas import tpu as pltpu
from jax.sharding import PartitionSpec as P

MESH = pl.DeviceIdType.MESH
F32 = jnp.float32
BF16 = jnp.bfloat16
LANES = 128
PAIR_CHUNKS = 8
EARLY_CHUNKS = 4
BIAS_ROWS = 8
TILE = 256


def flip(index, mask):
    out = index
    bit = 1
    while bit <= mask:
        if mask & bit:
            out = out + bit - 2 * bit * lax.rem(index // bit, 2)
        bit *= 2
    return out


def far_first(count):
    return sorted(range(1, count), key=lambda m: (-bin(m).count("1"), m))


def norm(values, gain_row):
    mean_value = jnp.mean(values, axis=-1, keepdims=True)
    centered = values - mean_value
    variance = jnp.mean(centered * centered, axis=-1, keepdims=True)
    scaled = centered * lax.rsqrt(variance + 1e-05)
    return scaled if gain_row is None else scaled * gain_row


def dot(a, b):
    return jnp.dot(a, b, preferred_element_type=F32)


def dot_nt(a, b):
    return lax.dot_general(a, b, (((1,), (1,)), ((), ())), preferred_element_type=F32)


def step_kernel(
    n_aa,
    n_ba,
    atom_hbm,
    noisy_ref,
    noise_ref,
    ids_ref,
    tok_hbm,
    pair_hbm,
    bias_w_ref,
    gains_ref,
    w_pos_ref,
    wat_hbm,
    wqg_hbm,
    wkv_hbm,
    wo_hbm,
    wup_hbm,
    wdn_hbm,
    wta_hbm,
    w_pos_out_ref,
    den_ref,
    tok_out_hbm,
    v_state,
    v_post,
    v_onehot,
    v_tok,
    v_pair,
    v_bias,
    v_wat,
    v_wqg,
    v_wkv,
    v_wo,
    v_wup,
    v_wdn,
    v_wta,
    ids_all,
    sum_send,
    sum_recv,
    rows_own,
    rows_z,
    rows_kv,
    q_own,
    q_all,
    v_km,
    v_vm,
    v_p,
    o_send,
    o_recv,
    st_send,
    st_recv,
    v_inner,
    t_own,
    t_all,
    ta_own,
    ta_all,
    load_sem,
    pair_sem,
    ids_sems,
    sum_sems,
    z_sems,
    kv_send,
    kv_recv,
    kv_local,
    q_sems,
    o_sems,
    st_sems,
    t_sems,
    ta_sems,
    out_sem,
):
    atoms = ids_ref.shape[1]
    atoms_pad = v_state.shape[0]
    tok_rows, cols, channels = v_pair.shape
    heads = bias_w_ref.shape[0]
    own, width = v_tok.shape
    head_dim = width // heads
    hidden = v_wdn.shape[0]
    per = tok_rows // cols
    pieces = cols // own
    me_a = lax.axis_index("aa")
    me_b = lax.axis_index("ba")

    barrier = pltpu.get_barrier_semaphore()
    for x in range(1, n_ba):
        pl.semaphore_signal(barrier, inc=1, device_id={"ba": flip(me_b, x)}, device_id_type=MESH)
    for x in range(1, n_aa):
        pl.semaphore_signal(barrier, inc=1, device_id={"aa": flip(me_a, x)}, device_id_type=MESH)

    own_start = pl.multiple_of(me_b * own, own)
    loads = {}
    for slot, (name, src, dst) in enumerate(
        [
            ("atom", atom_hbm, v_state.at[pl.ds(0, atoms)]),
            ("wat", wat_hbm, v_wat),
            ("tok", tok_hbm.at[pl.ds(own_start, own)], v_tok),
            ("wqg", wqg_hbm, v_wqg),
            ("wkv", wkv_hbm, v_wkv),
            ("wo", wo_hbm, v_wo),
            ("wup", wup_hbm, v_wup),
            ("wdn", wdn_hbm, v_wdn),
            ("wta", wta_hbm, v_wta),
        ]
    ):
        loads[name] = pltpu.make_async_copy(src, dst, load_sem.at[slot])
    step = tok_rows // PAIR_CHUNKS
    pair_loads = [
        pltpu.make_async_copy(
            pair_hbm.at[pl.ds(c * step, step)], v_pair.at[pl.ds(c * step, step)], pair_sem.at[c]
        )
        for c in range(PAIR_CHUNKS)
    ]
    for name in ("atom", "wat", "tok", "wqg"):
        loads[name].start()
    for copy in pair_loads:
        copy.start()
    for name in ("wkv", "wo", "wup", "wdn", "wta"):
        loads[name].start()

    def ba_copy(src, dst, sems, x):
        return pltpu.make_async_remote_copy(
            src_ref=src,
            dst_ref=dst,
            send_sem=sems.at[0, x - 1],
            recv_sem=sems.at[1, x - 1],
            device_id={"ba": flip(me_b, x)},
            device_id_type=MESH,
        )

    order = far_first(n_ba)

    sigma = jnp.full((3, atoms), noise_ref[0], F32)
    inv_scale = 1.0 / jnp.sqrt(sigma * sigma + 1.0)
    local_ids = ids_ref[...] - me_a * tok_rows
    v_post[...] = jnp.full(v_post.shape, -1.0, F32)
    v_post[0:3, 0:atoms] = noisy_ref[...] * inv_scale
    v_post[3:4, 0:atoms] = local_ids.astype(F32)
    ids_row = v_post[3:4, :]
    columns = v_post[...].T
    if atoms_pad > atoms:
        v_state[pl.ds(atoms, atoms_pad - atoms), :] = jnp.zeros(
            (atoms_pad - atoms, channels), F32
        )
    loads["atom"].wait()
    state = v_state[...]
    for c in range(3):
        state = state + columns[:, c : c + 1] * w_pos_ref[c : c + 1, :]
    v_state[...] = state
    lane_id = lax.broadcasted_iota(jnp.int32, (atoms_pad, tok_rows), 1).astype(F32)
    v_onehot[...] = jnp.where(columns[:, 3:4] == lane_id, 1.0, 0.0).astype(BF16)
    row_id = lax.broadcasted_iota(jnp.int32, (tok_rows, atoms_pad), 0).astype(F32)
    selector = jnp.where(row_id == ids_row, 1.0, 0.0).astype(BF16)
    loads["wat"].wait()
    hidden_atom = jnp.maximum(dot(state.astype(BF16), v_wat[...]), 0.0).astype(BF16)
    partial_sums = dot(selector, hidden_atom).astype(BF16)
    sum_send[...] = partial_sums.reshape(n_ba, own, width)

    pl.semaphore_wait(barrier, n_ba - 1 + n_aa - 1)
    ids_copies = {x: ba_copy(ids_ref, ids_all.at[x - 1], ids_sems, x) for x in order}
    sum_copies = {
        x: ba_copy(sum_send.at[flip(me_b, x)], sum_recv.at[x - 1], sum_sems, x) for x in order
    }
    for x in order:
        ids_copies[x].start()
        sum_copies[x].start()

    bias_w = bias_w_ref[...]

    def bias_chunk(c):
        pair_loads[c].wait()

        def rows(r, carry):
            start = c * step + r * BIAS_ROWS
            block = v_pair[pl.ds(start, BIAS_ROWS)].reshape(BIAS_ROWS * cols, channels)
            out = dot_nt(bias_w, block)
            for i in range(BIAS_ROWS):
                where = pl.multiple_of((start + i) * heads, heads)
                v_bias[pl.ds(where, heads), :] = out[:, i * cols : (i + 1) * cols]
            return carry

        lax.fori_loop(0, step // BIAS_ROWS, rows, 0)

    for c in range(EARLY_CHUNKS):
        bias_chunk(c)

    first_row = me_a * tok_rows + me_b * own
    own_row = lax.broadcasted_iota(jnp.int32, (own, atoms), 0) + first_row
    hits = jnp.where(own_row == ids_ref[...], 1.0, 0.0)
    summed = sum_send[me_b].astype(F32)
    for x in order:
        ids_copies[x].wait_recv()
        hits = hits + jnp.where(own_row == ids_all[x - 1], 1.0, 0.0)
    counts = jnp.sum(hits, axis=1, keepdims=True)
    for x in order:
        sum_copies[x].wait_recv()
        summed = summed + sum_recv[x - 1].astype(F32)
    loads["tok"].wait()
    tokens_start = v_tok[...] + summed / counts
    v_tok[...] = tokens_start
    normed = norm(tokens_start, gains_ref[0:1, :]).astype(BF16)
    rows_own[...] = normed

    z_order = far_first(n_aa)
    z_copies = {
        x: pltpu.make_async_remote_copy(
            src_ref=rows_own,
            dst_ref=rows_z.at[x - 1],
            send_sem=z_sems.at[0, x - 1],
            recv_sem=z_sems.at[1, x - 1],
            device_id={"aa": flip(me_a, x)},
            device_id_type=MESH,
        )
        for x in z_order
    }
    for x in z_order:
        z_copies[x].start()

    def forward(x):
        src = rows_own if x == 0 else rows_z.at[x - 1]
        group = flip(me_a, x)
        target = group * per + me_b // pieces
        dst = rows_kv.at[lax.rem(me_b, pieces)]
        remote = pltpu.make_async_remote_copy(
            src_ref=src,
            dst_ref=dst,
            send_sem=kv_send.at[x],
            recv_sem=kv_recv.at[lax.rem(me_b, pieces)],
            device_id={"ba": target},
            device_id_type=MESH,
        )
        local = pltpu.make_async_copy(src, dst, kv_local)
        return target, remote, local

    def start_forward(x):
        target, remote, local = forward(x)

        @pl.when(target != me_b)
        def _():
            remote.start()

        @pl.when(target == me_b)
        def _():
            local.start()

    start_forward(0)
    loads["wqg"].wait()
    query = dot(normed, v_wqg[:, 0:width]).astype(BF16)
    q_own[...] = query
    q_all[me_b] = query
    q_copies = {x: ba_copy(q_own, q_all.at[me_b], q_sems, x) for x in order}
    for x in order:
        q_copies[x].start()
    gate = jax.nn.sigmoid(dot(normed, v_wqg[:, width : 2 * width])).astype(BF16)

    for c in range(EARLY_CHUNKS, PAIR_CHUNKS):
        bias_chunk(c)
    for x in reversed(z_order):
        z_copies[x].wait_recv()
        start_forward(x)
    loads["wkv"].wait()
    for s in range(pieces):
        source = pieces * lax.rem(me_b, per) + s

        @pl.when(source == me_b)
        def _():
            pltpu.make_async_copy(rows_own, rows_kv.at[s], kv_local).wait()

        @pl.when(source != me_b)
        def _():
            pltpu.make_async_remote_copy(
                src_ref=rows_own,
                dst_ref=rows_kv.at[s],
                send_sem=kv_send.at[0],
                recv_sem=kv_recv.at[s],
                device_id={"ba": source},
                device_id_type=MESH,
            ).wait_recv()

    key_value = dot(rows_kv[...].reshape(cols, width), v_wkv[...]).astype(BF16)
    keys, values = key_value[:, :width], key_value[:, width:]
    spans = []
    for h in range(heads):
        lo = h * head_dim // LANES * LANES
        hi = ((h + 1) * head_dim + LANES - 1) // LANES * LANES
        spans.append((lo, hi))
        lane = lax.broadcasted_iota(jnp.int32, (cols, hi - lo), 1) + lo
        mine = (lane >= h * head_dim) & (lane < (h + 1) * head_dim)
        v_km[h, :, 0 : hi - lo] = jnp.where(mine, keys[:, lo:hi].astype(F32), 0.0).astype(BF16)
    tiles = []
    for t in range(width // TILE):
        h0 = t * TILE // head_dim
        h1 = (t * TILE + TILE - 1) // head_dim
        tiles.append((h0, h1))
        part = values[:, t * TILE : (t + 1) * TILE].astype(F32)
        lane = lax.broadcasted_iota(jnp.int32, (cols, TILE), 1) + t * TILE
        for h in range(h0, h1 + 1):
            mine = (lane >= h * head_dim) & (lane < (h + 1) * head_dim)
            v_vm[t, (h - h0) * cols : (h - h0 + 1) * cols, :] = jnp.where(mine, part, 0.0).astype(
                BF16
            )

    for x in order:
        q_copies[x].wait_recv()

    scale = head_dim ** (-0.5)
    rows2 = 2 * own
    lane = lax.broadcasted_iota(jnp.int32, (rows2, LANES), 1)
    groups = own // 8
    o_copies = {x: ba_copy(o_send.at[flip(me_b, x)], o_recv.at[x - 1], o_sems, x) for x in order}
    st_copies = {
        x: ba_copy(st_send.at[flip(me_b, x)], st_recv.at[x - 1], st_sems, x) for x in order
    }
    for d in far_first(n_ba // 2) + [0]:
        duo = flip(me_b // 2, d)
        stats = jnp.zeros((rows2, LANES), F32)
        q_rows = q_all[pl.ds(2 * duo, 2)].reshape(rows2, width)
        for h in range(heads):
            lo, hi = spans[h]
            scores = dot_nt(q_rows[:, lo:hi], v_km[h, :, 0 : hi - lo]) * scale
            scores = scores + v_bias[pl.ds(duo * (rows2 * heads) + h, rows2, stride=heads), :]
            top = jnp.max(scores, axis=1, keepdims=True)
            weights = jnp.exp(scores - top)
            total = jnp.sum(weights, axis=1, keepdims=True)
            stats = jnp.where(lane == h, top, stats)
            stats = jnp.where(lane == heads + h, total, stats)
            v_p[:, h * cols : (h + 1) * cols] = weights.astype(BF16)
        for t, (h0, h1) in enumerate(tiles):
            out = dot(
                v_p[:, h0 * cols : (h1 + 1) * cols], v_vm[t, 0 : (h1 - h0 + 1) * cols, :]
            )
            o_send[pl.ds(2 * duo, 2), :, t * TILE : (t + 1) * TILE] = out.astype(BF16).reshape(
                2, own, TILE
            )
        for c in range(2):
            packed = stats[c * own : c * own + 8]
            for g in range(1, groups):
                piece = pltpu.roll(stats[c * own + 8 * g : c * own + 8 * g + 8], 2 * heads * g, 1)
                packed = jnp.where(lane[0:8] >= 2 * heads * g, piece, packed)
            st_send[2 * duo + c] = packed
        for x in (2 * d + 1, 2 * d):
            if x:
                st_copies[x].start()
                o_copies[x].start()

    def unpack(packed):
        parts = [packed]
        for g in range(1, groups):
            parts.append(pltpu.roll(packed, LANES - 2 * heads * g, 1))
        return jnp.concatenate(parts, axis=0)

    tops = [unpack(st_send[me_b])]
    for x in range(1, n_ba):
        st_copies[x].wait_recv()
        tops.append(unpack(st_recv[x - 1]))
    overall = tops[0]
    for top in tops[1:]:
        overall = jnp.maximum(overall, top)
    factors = [jnp.exp(top - overall) for top in tops]
    denominator = jnp.zeros((own, LANES), F32)
    for factor, top in zip(factors, tops):
        denominator = denominator + factor * pltpu.roll(top, LANES - heads, 1)
    head_row = lax.broadcasted_iota(jnp.int32, (LANES, width), 0)
    head_lane = lax.broadcasted_iota(jnp.int32, (LANES, width), 1)
    inside = (head_lane >= head_row * head_dim) & (head_lane < (head_row + 1) * head_dim)
    spread = jnp.where(inside, 1.0, 0.0).astype(BF16)
    live = lane[0:own] < heads
    shares = jnp.concatenate(
        [jnp.where(live, factor / denominator, 0.0) for factor in factors], axis=0
    )
    coarse = shares.astype(BF16)
    fine = (shares - coarse.astype(F32)).astype(BF16)
    wide = dot(coarse, spread) + dot(fine, spread)
    attended = wide[0:own] * o_send[me_b].astype(F32)
    for x in range(1, n_ba):
        o_copies[x].wait_recv()
        attended = attended + wide[x * own : (x + 1) * own] * o_recv[x - 1].astype(F32)
    mixed = (attended * gate.astype(F32)).astype(BF16)
    loads["wo"].wait()
    tokens_mid = v_tok[...] + dot(mixed, v_wo[...])
    normed_mid = norm(tokens_mid, gains_ref[1:2, :]).astype(BF16)
    loads["wup"].wait()
    part = 512
    for n in range(0, hidden, part):
        first = dot(normed_mid, v_wup[:, n : n + part])
        second = dot(normed_mid, v_wup[:, hidden + n : hidden + n + part])
        v_inner[:, n : n + part] = (first * jax.nn.sigmoid(first) * second).astype(BF16)
    loads["wdn"].wait()
    token_out = tokens_mid + dot(v_inner[...], v_wdn[...])
    token_round = token_out.astype(BF16)
    t_own[...] = token_round
    t_all[me_b] = token_round
    t_copies = {x: ba_copy(t_own, t_all.at[me_b], t_sems, x) for x in order}
    for x in order:
        t_copies[x].start()
    loads["wta"].wait()
    normed_out = norm(token_out, gains_ref[2:3, :]).astype(BF16)
    token_atom = dot(normed_out, v_wta[...]).astype(BF16)
    ta_own[...] = token_atom
    ta_all[me_b] = token_atom
    ta_copies = {x: ba_copy(ta_own, ta_all.at[me_b], ta_sems, x) for x in order}
    for x in order:
        ta_copies[x].start()
    for x in order:
        ta_copies[x].wait_recv()
    picked = dot(v_onehot[...], ta_all[...].reshape(tok_rows, channels))
    atom_normed = norm(v_state[...] + picked, None).astype(BF16)
    update = dot_nt(w_pos_out_ref[...], atom_normed)[:, 0:atoms]
    den_ref[...] = noisy_ref[...] * (inv_scale * inv_scale) + update * (sigma * inv_scale)
    for x in order:
        t_copies[x].wait_recv()
    result = pltpu.make_async_copy(t_all, tok_out_hbm, out_sem)
    result.start()
    for x in order:
        for copies in (ids_copies, sum_copies, q_copies, st_copies, o_copies, t_copies, ta_copies):
            copies[x].wait_send()
    for x in z_order:
        z_copies[x].wait_send()
    for x in range(n_aa):
        target, remote, _ = forward(x)

        @pl.when(target != me_b)
        def _():
            remote.wait_send()

    result.wait()


def on_device(
    n_aa,
    n_ba,
    atom_cond,
    noisy_pos,
    noise_level,
    atom_token,
    token_cond,
    pair,
    pair_bias_weight,
    gains,
    w_pos,
    w_atom_token,
    w_query_gate,
    w_key_value,
    w_attn_out,
    w_up,
    w_down,
    w_token_atom,
    w_pos_out,
):
    atoms, channels = atom_cond.shape
    atoms_pad = -(-atoms // LANES) * LANES
    tok_rows, width = token_cond.shape
    cols = pair.shape[1]
    heads = pair_bias_weight.shape[0]
    own = tok_rows // n_ba
    pieces = cols // own
    head_dim = width // heads
    tile_heads = max(
        (t * TILE + TILE - 1) // head_dim - t * TILE // head_dim + 1 for t in range(width // TILE)
    )
    vmem = pl.BlockSpec(memory_space=pltpu.VMEM)
    smem = pl.BlockSpec(memory_space=pltpu.SMEM)
    hbm = pl.BlockSpec(memory_space=pl.ANY)
    dma = pltpu.SemaphoreType.DMA
    denoised, tokens = pl.pallas_call(
        functools.partial(step_kernel, n_aa, n_ba),
        out_shape=[
            jax.ShapeDtypeStruct((3, atoms), F32),
            jax.ShapeDtypeStruct((n_ba, own, width), BF16),
        ],
        in_specs=[hbm, vmem, smem, vmem, hbm, hbm, vmem, vmem, vmem] + [hbm] * 7 + [vmem],
        out_specs=[vmem, hbm],
        scratch_shapes=[
            pltpu.VMEM((atoms_pad, channels), F32),
            pltpu.VMEM((LANES, atoms_pad), F32),
            pltpu.VMEM((atoms_pad, tok_rows), BF16),
            pltpu.VMEM((own, width), F32),
            pltpu.VMEM(pair.shape, BF16),
            pltpu.VMEM((tok_rows * heads, cols), F32),
            pltpu.VMEM(w_atom_token.shape, BF16),
            pltpu.VMEM(w_query_gate.shape, BF16),
            pltpu.VMEM(w_key_value.shape, BF16),
            pltpu.VMEM(w_attn_out.shape, BF16),
            pltpu.VMEM(w_up.shape, BF16),
            pltpu.VMEM(w_down.shape, BF16),
            pltpu.VMEM(w_token_atom.shape, BF16),
            pltpu.VMEM((n_ba - 1, 1, atoms), jnp.int32),
            pltpu.VMEM((n_ba, own, width), BF16),
            pltpu.VMEM((n_ba - 1, own, width), BF16),
            pltpu.VMEM((own, width), BF16),
            pltpu.VMEM((n_aa - 1, own, width), BF16),
            pltpu.VMEM((pieces, own, width), BF16),
            pltpu.VMEM((own, width), BF16),
            pltpu.VMEM((n_ba, own, width), BF16),
            pltpu.VMEM((heads, cols, 2 * LANES), BF16),
            pltpu.VMEM((width // TILE, tile_heads * cols, TILE), BF16),
            pltpu.VMEM((2 * own, heads * cols), BF16),
            pltpu.VMEM((n_ba, own, width), BF16),
            pltpu.VMEM((n_ba - 1, own, width), BF16),
            pltpu.VMEM((n_ba, 8, LANES), F32),
            pltpu.VMEM((n_ba - 1, 8, LANES), F32),
            pltpu.VMEM((own, w_down.shape[0]), BF16),
            pltpu.VMEM((own, width), BF16),
            pltpu.VMEM((n_ba, own, width), BF16),
            pltpu.VMEM((own, channels), BF16),
            pltpu.VMEM((n_ba, own, channels), BF16),
            dma((9,)),
            dma((PAIR_CHUNKS,)),
            dma((2, n_ba - 1)),
            dma((2, n_ba - 1)),
            dma((2, n_aa - 1)),
            dma((n_aa,)),
            dma((pieces,)),
            dma,
            dma((2, n_ba - 1)),
            dma((2, n_ba - 1)),
            dma((2, n_ba - 1)),
            dma((2, n_ba - 1)),
            dma((2, n_ba - 1)),
            dma,
        ],
        compiler_params=pltpu.CompilerParams(
            collective_id=0, has_side_effects=True, vmem_limit_bytes=56 * 1024 * 1024
        ),
    )(
        atom_cond,
        noisy_pos,
        noise_level,
        atom_token.reshape(1, -1),
        token_cond,
        pair,
        pair_bias_weight,
        gains,
        w_pos,
        w_atom_token,
        w_query_gate,
        w_key_value,
        w_attn_out,
        w_up,
        w_down,
        w_token_atom,
        w_pos_out,
    )
    return denoised, tokens.reshape(tok_rows, width).astype(F32)


def solution(mesh):
    in_specs = (
        P(("aa", "ba"), None),
        P(None, ("aa", "ba")),
        P(),
        P(("aa", "ba")),
        P("aa", None),
        P("aa", "ba", None),
    ) + (P(),) * 11
    out_specs = (P(None, ("aa", "ba")), P("aa", None))
    return jax.shard_map(
        functools.partial(on_device, mesh.shape["aa"], mesh.shape["ba"]),
        mesh=mesh,
        in_specs=in_specs,
        out_specs=out_specs,
        check_vma=False,
    )
```

```python
import functools

import jax
import jax.numpy as jnp
from jax import lax
from jax.experimental import pallas as pl
from jax.experimental.pallas import tpu as pltpu
from jax.sharding import PartitionSpec as P

MESH = pl.DeviceIdType.MESH
F32 = jnp.float32
BF16 = jnp.bfloat16
LANES = 128
PAIR_CHUNKS = 8
EARLY_CHUNKS = 4
BIAS_ROWS = 8


def flip(index, mask):
    out = index
    bit = 1
    while bit <= mask:
        if mask & bit:
            out = out + bit - 2 * bit * lax.rem(index // bit, 2)
        bit *= 2
    return out


def far_first(count):
    return sorted(range(1, count), key=lambda m: (-bin(m).count("1"), m))


def norm(values, gain_row):
    mean_value = jnp.mean(values, axis=-1, keepdims=True)
    centered = values - mean_value
    variance = jnp.mean(centered * centered, axis=-1, keepdims=True)
    scaled = centered * lax.rsqrt(variance + 1e-05)
    return scaled if gain_row is None else scaled * gain_row


def dot(a, b):
    return jnp.dot(a, b, preferred_element_type=F32)


def dot_nt(a, b):
    return lax.dot_general(a, b, (((1,), (1,)), ((), ())), preferred_element_type=F32)


def step_kernel(
    n_aa,
    n_ba,
    atom_hbm,
    noisy_ref,
    noise_ref,
    ids_hbm,
    tok_hbm,
    pair_hbm,
    bias_w_ref,
    gains_ref,
    w_pos_ref,
    wat_hbm,
    wqg_hbm,
    wkv_hbm,
    wo_hbm,
    wup_hbm,
    wdn_hbm,
    wta_hbm,
    w_pos_out_ref,
    den_ref,
    t_all,
    v_state,
    v_post,
    v_onehot,
    v_tok,
    v_pair,
    v_bias,
    bias_send,
    v_wat,
    v_wqg,
    v_wkv,
    v_wo,
    v_wup,
    v_wdn,
    v_wta,
    v_ids,
    ids_all,
    state_own,
    state_mate,
    sum_send,
    sum_recv,
    rows_own,
    rows_kv,
    q_own,
    q_all,
    v_km,
    v_vm,
    v_p,
    o_send,
    o_recv,
    st_send,
    st_recv,
    v_inner,
    t_own,
    ta_own,
    ta_all,
    load_sem,
    pair_sem,
    ids_sems,
    state_sems,
    sum_sems,
    bias_sems,
    kv_send,
    kv_recv,
    kv_local,
    kvm_sems,
    q_sems,
    o_sems,
    st_sems,
    t_sems,
    tm_sems,
    ta_sems,
):
    atoms = noisy_ref.shape[1]
    atoms_pad = v_state.shape[0]
    tok_rows, cols, channels = v_pair.shape
    heads = bias_w_ref.shape[0]
    half = heads // 2
    own, width = v_tok.shape
    head_dim = width // heads
    span = width // 2
    hidden = v_wdn.shape[0]
    chips = n_ba // 2
    keys_n = 2 * cols
    me_a = lax.axis_index("aa")
    me_b = lax.axis_index("ba")
    core = lax.rem(me_b, 2)
    chip = me_b // 2

    def at(a, b):
        return {"aa": a, "ba": b}

    def greet(device):
        pl.semaphore_signal(barrier, inc=1, device_id=device, device_id_type=MESH)

    barrier = pltpu.get_barrier_semaphore()
    for x in range(1, n_ba):
        greet(at(me_a, flip(me_b, x)))
    for x in range(1, n_aa):
        greet(at(flip(me_a, x), 2 * me_a + core))
    for x in range(1, chips):
        greet(at(chip, flip(me_b, 2 * x)))

    @pl.when(chip != me_a)
    def _():
        greet(at(me_a, 2 * me_a + core))
        greet(at(chip, me_b))

    greetings = n_ba - 1 + n_aa - 1 + chips - 1 + jnp.where(chip != me_a, 2, 0)

    if atoms_pad > atoms:
        v_state[pl.ds(atoms, atoms_pad - atoms), :] = jnp.zeros(
            (atoms_pad - atoms, channels), F32
        )
    own_start = pl.multiple_of(me_b * own, own)
    span_start = pl.multiple_of(core * span, LANES)
    loads = {}
    for slot, (name, src, dst) in enumerate(
        [
            ("ids", ids_hbm, v_ids.at[0]),
            ("atom", atom_hbm, v_state.at[pl.ds(0, atoms)]),
            ("wat", wat_hbm, v_wat),
            ("tok", tok_hbm.at[pl.ds(own_start, own)], v_tok),
            ("wqg", wqg_hbm, v_wqg),
            ("wk", wkv_hbm.at[:, pl.ds(span_start, span)], v_wkv.at[:, pl.ds(0, span)]),
            (
                "wv",
                wkv_hbm.at[:, pl.ds(pl.multiple_of(width + core * span, LANES), span)],
                v_wkv.at[:, pl.ds(span, span)],
            ),
            ("wo", wo_hbm, v_wo),
            ("wup", wup_hbm, v_wup),
            ("wdn", wdn_hbm, v_wdn),
            ("wta", wta_hbm, v_wta),
        ]
    ):
        loads[name] = pltpu.make_async_copy(src, dst, load_sem.at[slot])
    step = tok_rows // PAIR_CHUNKS
    pair_loads = [
        pltpu.make_async_copy(
            pair_hbm.at[pl.ds(c * step, step)], v_pair.at[pl.ds(c * step, step)], pair_sem.at[c]
        )
        for c in range(PAIR_CHUNKS)
    ]
    for name in ("ids", "atom", "wat", "tok"):
        loads[name].start()
    for copy in pair_loads:
        copy.start()
    for name in ("wqg", "wk", "wv", "wo", "wup", "wdn", "wta"):
        loads[name].start()

    def ba_copy(src, dst, sems, x, slot):
        return pltpu.make_async_remote_copy(
            src_ref=src,
            dst_ref=dst,
            send_sem=sems.at[0, slot],
            recv_sem=sems.at[1, slot],
            device_id=at(me_a, flip(me_b, x)),
            device_id_type=MESH,
        )

    order = far_first(n_ba)
    chip_order = far_first(chips)
    sent = []

    def send(copy):
        copy.start()
        sent.append(copy)

    sigma = jnp.full((3, atoms), noise_ref[0], F32)
    inv_scale = 1.0 / jnp.sqrt(sigma * sigma + 1.0)
    v_post[...] = jnp.full(v_post.shape, -1.0, F32)
    v_post[0:3, 0:atoms] = noisy_ref[...] * inv_scale
    loads["ids"].wait()
    ids_row = v_ids[...]
    v_post[3:4, :] = ids_row.astype(F32)
    columns = v_post[...].T
    loads["atom"].wait()
    state = v_state[...]
    for c in range(3):
        state = state + columns[:, c : c + 1] * w_pos_ref[c : c + 1, :]
    v_state[...] = state
    rounded = state.astype(BF16)
    state_own[...] = rounded

    pl.semaphore_wait(barrier, greetings)
    state_copy = ba_copy(state_own, state_mate, state_sems, 1, 0)
    send(state_copy)
    ids_copies = {x: ba_copy(v_ids, ids_all.at[x - 1], ids_sems, x, x - 1) for x in order}
    for x in [1] + [x for x in order if x != 1]:
        send(ids_copies[x])

    def select(ids):
        row = lax.broadcasted_iota(jnp.int32, (chips * own, atoms_pad), 0)
        token = row + own * (row // own) + (own * core + me_a * tok_rows)
        return jnp.where(token == ids, 1.0, 0.0).astype(BF16)

    loads["wat"].wait()
    hidden_atom = jnp.maximum(dot(rounded, v_wat[...]), 0.0).astype(BF16)
    chip_sums = dot(select(ids_row), hidden_atom)
    ids_copies[1].wait_recv()
    selector = select(ids_all[0])
    state_copy.wait_recv()
    hidden_atom = jnp.maximum(dot(state_mate[...], v_wat[...]), 0.0).astype(BF16)
    chip_sums = chip_sums + dot(selector, hidden_atom)
    sum_send[...] = chip_sums.astype(BF16).reshape(chips, own, width)
    sum_copies = {
        d: ba_copy(sum_send.at[flip(chip, d)], sum_recv.at[d - 1], sum_sems, 2 * d, d - 1)
        for d in chip_order
    }
    for d in chip_order:
        send(sum_copies[d])

    lane_id = lax.broadcasted_iota(jnp.int32, (atoms_pad, tok_rows), 1) + me_a * tok_rows
    v_onehot[...] = jnp.where(columns[:, 3:4] == lane_id.astype(F32), 1.0, 0.0).astype(BF16)
    weights_all = bias_w_ref[...].astype(F32)
    first_half, second_half = weights_all[0:half], weights_all[half:heads]
    bias_w = jnp.concatenate(
        [
            jnp.where(core == 0, first_half, second_half),
            jnp.where(core == 0, second_half, first_half),
        ],
        axis=0,
    ).astype(BF16)
    bias_rows = step * half
    bias_copies = [
        ba_copy(
            bias_send.at[pl.ds(c * bias_rows, bias_rows)],
            v_bias.at[core, pl.ds(c * bias_rows, bias_rows)],
            bias_sems,
            1,
            c,
        )
        for c in range(PAIR_CHUNKS)
    ]

    def bias_chunk(c):
        pair_loads[c].wait()

        def rows(r, carry):
            start = c * step + r * BIAS_ROWS
            block = v_pair[pl.ds(start, BIAS_ROWS)].reshape(BIAS_ROWS * cols, channels)
            out = dot_nt(bias_w, block)
            for i in range(BIAS_ROWS):
                where = pl.ds(pl.multiple_of((start + i) * half, half), half)
                v_bias[core, where, :] = out[0:half, i * cols : (i + 1) * cols]
                bias_send[where, :] = out[half:heads, i * cols : (i + 1) * cols]
            return carry

        lax.fori_loop(0, step // BIAS_ROWS, rows, 0)
        send(bias_copies[c])

    for c in range(EARLY_CHUNKS):
        bias_chunk(c)

    own_row = lax.broadcasted_iota(jnp.int32, (own, atoms_pad), 0) + (
        me_a * tok_rows + me_b * own
    )
    hits = jnp.where(own_row == ids_row, 1.0, 0.0)
    for x in order:
        if x != 1:
            ids_copies[x].wait_recv()
        hits = hits + jnp.where(own_row == ids_all[x - 1], 1.0, 0.0)
    counts = jnp.sum(hits, axis=1, keepdims=True)
    summed = sum_send[chip].astype(F32)
    for d in chip_order:
        sum_copies[d].wait_recv()
        summed = summed + sum_recv[d - 1].astype(F32)
    loads["tok"].wait()
    tokens_start = v_tok[...] + summed / counts
    v_tok[...] = tokens_start
    normed = norm(tokens_start, gains_ref[0:1, :]).astype(BF16)
    rows_own[...] = normed

    def kv_copy(x):
        return pltpu.make_async_remote_copy(
            src_ref=rows_own,
            dst_ref=rows_kv.at[me_b],
            send_sem=kv_send.at[x],
            recv_sem=kv_recv.at[chip],
            device_id=at(flip(me_a, x), 2 * me_a + core),
            device_id_type=MESH,
        )

    own_piece = pltpu.make_async_copy(rows_own, rows_kv.at[me_b], kv_local)
    for x in far_first(n_aa):
        send(kv_copy(x))

    @pl.when(chip == me_a)
    def _():
        own_piece.start()

    @pl.when(chip != me_a)
    def _():
        kv_copy(0).start()

    loads["wqg"].wait()
    query = dot(normed, v_wqg[:, 0:width]).astype(BF16)
    for c in range(2):
        q_own[c] = query[:, c * span : (c + 1) * span]
    q_all[me_b] = q_own[core]
    q_copies = {
        x: ba_copy(q_own.at[lax.rem(core + x, 2)], q_all.at[me_b], q_sems, x, x - 1)
        for x in order
    }
    for x in order:
        send(q_copies[x])
    gate = jax.nn.sigmoid(dot(normed, v_wqg[:, width : 2 * width])).astype(BF16)

    for c in range(EARLY_CHUNKS, PAIR_CHUNKS):
        bias_chunk(c)
    mate_rows = {}
    for d in range(chips):
        piece = flip(me_b, 2 * d)
        source = pltpu.make_async_remote_copy(
            src_ref=rows_own,
            dst_ref=rows_kv.at[piece],
            send_sem=kv_send.at[0],
            recv_sem=kv_recv.at[flip(chip, d)],
            device_id=at(chip, piece),
            device_id_type=MESH,
        )
        if d == 0:

            @pl.when(chip == me_a)
            def _():
                own_piece.wait()

            @pl.when(chip != me_a)
            def _():
                source.wait_recv()
        else:
            source.wait_recv()
        mate_rows[d] = ba_copy(rows_kv.at[piece], rows_kv.at[piece], kvm_sems, 1, d)
        send(mate_rows[d])
    loads["wk"].wait()
    loads["wv"].wait()
    for d in range(chips):
        mate_rows[d].wait_recv()

    key_value = dot(rows_kv[...].reshape(keys_n, width), v_wkv[...])
    spans = []
    for h in range(half):
        lo = h * head_dim // LANES * LANES
        hi = ((h + 1) * head_dim + LANES - 1) // LANES * LANES
        spans.append((lo, hi))
        lane = lax.broadcasted_iota(jnp.int32, (keys_n, hi - lo), 1) + lo
        mine = (lane >= h * head_dim) & (lane < (h + 1) * head_dim)
        v_km[h, :, 0 : hi - lo] = jnp.where(mine, key_value[:, lo:hi], 0.0).astype(BF16)
    tiles = []
    for t in range(span // LANES):
        h0 = t * LANES // head_dim
        h1 = (t * LANES + LANES - 1) // head_dim
        tiles.append((h0, h1))
        part = key_value[:, span + t * LANES : span + (t + 1) * LANES]
        lane = lax.broadcasted_iota(jnp.int32, (keys_n, LANES), 1) + t * LANES
        for h in range(h0, h1 + 1):
            mine = (lane >= h * head_dim) & (lane < (h + 1) * head_dim)
            v_vm[t, (h - h0) * keys_n : (h - h0 + 1) * keys_n, :] = jnp.where(
                mine, part, 0.0
            ).astype(BF16)

    for x in order:
        q_copies[x].wait_recv()
    for c in range(PAIR_CHUNKS):
        bias_copies[c].wait_recv()

    scale = head_dim ** (-0.5)
    rows2 = 2 * own
    lane = lax.broadcasted_iota(jnp.int32, (rows2, LANES), 1)
    top_lane = lane - half * core
    groups = own // 8
    o_copies = {
        x: ba_copy(o_send.at[flip(me_b, x)], o_recv.at[x - 1], o_sems, x, x - 1) for x in order
    }
    st_copies = {
        x: ba_copy(st_send.at[flip(me_b, x)], st_recv.at[x - 1], st_sems, x, x - 1)
        for x in order
    }
    for d in chip_order + [0]:
        duo = flip(chip, d)
        stats = jnp.zeros((rows2, LANES), F32)
        q_rows = q_all[pl.ds(2 * duo, 2)].reshape(rows2, span)
        for h in range(half):
            lo, hi = spans[h]
            scores = dot_nt(q_rows[:, lo:hi], v_km[h, :, 0 : hi - lo]) * scale
            where = pl.ds(duo * (rows2 * half) + h, rows2, stride=half)
            parts = [
                scores[:, k * cols : (k + 1) * cols] + v_bias[k, where, :] for k in range(2)
            ]
            top = jnp.max(jnp.maximum(parts[0], parts[1]), axis=1, keepdims=True)
            parts = [jnp.exp(part - top) for part in parts]
            total = jnp.sum(parts[0] + parts[1], axis=1, keepdims=True)
            stats = jnp.where(top_lane == h, top, stats)
            stats = jnp.where(top_lane == heads + h, total, stats)
            for k in range(2):
                v_p[:, h * keys_n + k * cols : h * keys_n + (k + 1) * cols] = parts[k].astype(
                    BF16
                )
        for t, (h0, h1) in enumerate(tiles):
            out = dot(
                v_p[:, h0 * keys_n : (h1 + 1) * keys_n], v_vm[t, 0 : (h1 - h0 + 1) * keys_n, :]
            )
            o_send[pl.ds(2 * duo, 2), :, t * LANES : (t + 1) * LANES] = out.astype(BF16).reshape(
                2, own, LANES
            )
        for c in range(2):
            packed = stats[c * own : c * own + 8]
            for g in range(1, groups):
                piece = pltpu.roll(stats[c * own + 8 * g : c * own + 8 * g + 8], 2 * heads * g, 1)
                packed = jnp.where(lane[0:8] >= 2 * heads * g, piece, packed)
            st_send[2 * duo + c] = packed
        for x in (2 * d + 1, 2 * d):
            if x:
                send(st_copies[x])
                send(o_copies[x])

    def unpack(packed):
        parts = [packed]
        for g in range(1, groups):
            parts.append(pltpu.roll(packed, LANES - 2 * heads * g, 1))
        return jnp.concatenate(parts, axis=0)

    tops = []
    for d in range(chips):
        if d:
            st_copies[2 * d].wait_recv()
        st_copies[2 * d + 1].wait_recv()
        mine = st_recv[2 * d - 1] if d else st_send[me_b]
        tops.append(unpack(mine + st_recv[2 * d]))
    overall = tops[0]
    for top in tops[1:]:
        overall = jnp.maximum(overall, top)
    factors = [jnp.exp(top - overall) for top in tops]
    denominator = jnp.zeros((own, LANES), F32)
    for factor, top in zip(factors, tops):
        denominator = denominator + factor * pltpu.roll(top, LANES - heads, 1)
    head_row = lax.broadcasted_iota(jnp.int32, (LANES, width), 0)
    head_lane = lax.broadcasted_iota(jnp.int32, (LANES, width), 1)
    inside = (head_lane >= head_row * head_dim) & (head_lane < (head_row + 1) * head_dim)
    spread = jnp.where(inside, 1.0, 0.0).astype(BF16)
    live = lane[0:own] < heads
    shares = jnp.concatenate(
        [jnp.where(live, factor / denominator, 0.0) for factor in factors], axis=0
    )
    coarse = shares.astype(BF16)
    fine = (shares - coarse.astype(F32)).astype(BF16)
    wide = dot(coarse, spread) + dot(fine, spread)
    left = jnp.zeros((own, span), F32)
    right = jnp.zeros((own, span), F32)
    for d in range(chips):
        if d:
            o_copies[2 * d].wait_recv()
        o_copies[2 * d + 1].wait_recv()
        mine = (o_recv[2 * d - 1] if d else o_send[me_b]).astype(F32)
        other = o_recv[2 * d].astype(F32)
        part = wide[d * own : (d + 1) * own]
        left = left + part[:, 0:span] * jnp.where(core == 0, mine, other)
        right = right + part[:, span:width] * jnp.where(core == 0, other, mine)
    attended = jnp.concatenate([left, right], axis=1)
    mixed = (attended * gate.astype(F32)).astype(BF16)
    loads["wo"].wait()
    tokens_mid = v_tok[...] + dot(mixed, v_wo[...])
    normed_mid = norm(tokens_mid, gains_ref[1:2, :]).astype(BF16)
    loads["wup"].wait()
    part = 512
    for n in range(0, hidden, part):
        first = dot(normed_mid, v_wup[:, n : n + part])
        second = dot(normed_mid, v_wup[:, hidden + n : hidden + n + part])
        v_inner[:, n : n + part] = (first * jax.nn.sigmoid(first) * second).astype(BF16)
    loads["wdn"].wait()
    token_out = tokens_mid + dot(v_inner[...], v_wdn[...])
    token_round = token_out.astype(BF16)
    t_own[...] = token_round
    t_all[me_b] = token_round
    loads["wta"].wait()
    normed_out = norm(token_out, gains_ref[2:3, :]).astype(BF16)
    token_atom = dot(normed_out, v_wta[...]).astype(BF16)
    ta_own[...] = token_atom
    ta_all[me_b] = token_atom
    ta_copies = {x: ba_copy(ta_own, ta_all.at[me_b], ta_sems, x, x - 1) for x in order}
    for x in order:
        send(ta_copies[x])
    t_copies = {
        d: ba_copy(t_own, t_all.at[me_b], t_sems, 2 * d, d - 1) for d in chip_order
    }
    for d in chip_order:
        send(t_copies[d])
    tm_copies = {0: ba_copy(t_own, t_all.at[me_b], tm_sems, 1, 0)}
    send(tm_copies[0])
    for x in order:
        ta_copies[x].wait_recv()
    picked = dot(v_onehot[...], ta_all[...].reshape(tok_rows, channels))
    atom_normed = norm(v_state[...] + picked, None).astype(BF16)
    update = dot_nt(w_pos_out_ref[...], atom_normed)[:, 0:atoms]
    den_ref[...] = noisy_ref[...] * (inv_scale * inv_scale) + update * (sigma * inv_scale)
    for d in range(1, chips):
        piece = flip(me_b, 2 * d)
        t_copies[d].wait_recv()
        tm_copies[d] = ba_copy(t_all.at[piece], t_all.at[piece], tm_sems, 1, d)
        send(tm_copies[d])
    for d in range(chips):
        tm_copies[d].wait_recv()
    for copy in sent:
        copy.wait_send()

    @pl.when(chip != me_a)
    def _():
        kv_copy(0).wait_send()


def finish_kernel(tok_ref, den_ref, den_out_ref, tok_out_ref):
    den_out_ref[...] = den_ref[...]
    tok_out_ref[...] = tok_ref[...].astype(F32)


def on_device(
    n_aa,
    n_ba,
    atom_cond,
    noisy_pos,
    noise_level,
    atom_token,
    token_cond,
    pair,
    pair_bias_weight,
    gains,
    w_pos,
    w_atom_token,
    w_query_gate,
    w_key_value,
    w_attn_out,
    w_up,
    w_down,
    w_token_atom,
    w_pos_out,
):
    atoms, channels = atom_cond.shape
    atoms_pad = -(-atoms // LANES) * LANES
    tok_rows, width = token_cond.shape
    cols = pair.shape[1]
    heads = pair_bias_weight.shape[0]
    own = tok_rows // n_ba
    chips = n_ba // 2
    half, span, keys_n = heads // 2, width // 2, 2 * cols
    head_dim = width // heads
    if tok_rows != 2 * cols or chips != n_aa:
        raise ValueError("unsupported mesh")
    tile_heads = max(
        (t * LANES + LANES - 1) // head_dim - t * LANES // head_dim + 1
        for t in range(span // LANES)
    )
    ids = atom_token
    if atoms_pad > atoms:
        ids = jnp.pad(atom_token, (0, atoms_pad - atoms), constant_values=-1)
    vmem = pl.BlockSpec(memory_space=pltpu.VMEM)
    smem = pl.BlockSpec(memory_space=pltpu.SMEM)
    hbm = pl.BlockSpec(memory_space=pltpu.HBM)
    dma = pltpu.SemaphoreType.DMA
    operands = [
        pltpu.with_memory_space_constraint(value, pltpu.HBM) if value.size > 1 else value
        for value in (
            atom_cond,
            noisy_pos,
            noise_level,
            ids,
            token_cond,
            pair,
            pair_bias_weight,
            gains,
            w_pos,
            w_atom_token,
            w_query_gate,
            w_key_value,
            w_attn_out,
            w_up,
            w_down,
            w_token_atom,
            w_pos_out,
        )
    ]
    denoised, tokens = pl.pallas_call(
        functools.partial(step_kernel, n_aa, n_ba),
        out_shape=[
            jax.ShapeDtypeStruct((3, atoms), F32),
            jax.ShapeDtypeStruct((n_ba, own, width), BF16),
        ],
        in_specs=[hbm, vmem, smem, hbm, hbm, hbm, vmem, vmem, vmem] + [hbm] * 7 + [vmem],
        out_specs=[vmem, vmem],
        scratch_shapes=[
            pltpu.VMEM((atoms_pad, channels), F32),
            pltpu.VMEM((LANES, atoms_pad), F32),
            pltpu.VMEM((atoms_pad, tok_rows), BF16),
            pltpu.VMEM((own, width), F32),
            pltpu.VMEM(pair.shape, BF16),
            pltpu.VMEM((2, tok_rows * half, cols), F32),
            pltpu.VMEM((tok_rows * half, cols), F32),
            pltpu.VMEM(w_atom_token.shape, BF16),
            pltpu.VMEM(w_query_gate.shape, BF16),
            pltpu.VMEM((width, width), BF16),
            pltpu.VMEM(w_attn_out.shape, BF16),
            pltpu.VMEM(w_up.shape, BF16),
            pltpu.VMEM(w_down.shape, BF16),
            pltpu.VMEM(w_token_atom.shape, BF16),
            pltpu.VMEM((1, atoms_pad), jnp.int32),
            pltpu.VMEM((n_ba - 1, 1, atoms_pad), jnp.int32),
            pltpu.VMEM((atoms_pad, channels), BF16),
            pltpu.VMEM((atoms_pad, channels), BF16),
            pltpu.VMEM((chips, own, width), BF16),
            pltpu.VMEM((chips - 1, own, width), BF16),
            pltpu.VMEM((own, width), BF16),
            pltpu.VMEM((n_ba, own, width), BF16),
            pltpu.VMEM((2, own, span), BF16),
            pltpu.VMEM((n_ba, own, span), BF16),
            pltpu.VMEM((half, keys_n, 2 * LANES), BF16),
            pltpu.VMEM((span // LANES, tile_heads * keys_n, LANES), BF16),
            pltpu.VMEM((2 * own, half * keys_n), BF16),
            pltpu.VMEM((n_ba, own, span), BF16),
            pltpu.VMEM((n_ba - 1, own, span), BF16),
            pltpu.VMEM((n_ba, 8, LANES), F32),
            pltpu.VMEM((n_ba - 1, 8, LANES), F32),
            pltpu.VMEM((own, w_down.shape[0]), BF16),
            pltpu.VMEM((own, width), BF16),
            pltpu.VMEM((own, channels), BF16),
            pltpu.VMEM((n_ba, own, channels), BF16),
            dma((11,)),
            dma((PAIR_CHUNKS,)),
            dma((2, n_ba - 1)),
            dma((2, 1)),
            dma((2, chips - 1)),
            dma((2, PAIR_CHUNKS)),
            dma((n_aa,)),
            dma((chips,)),
            dma,
            dma((2, chips)),
            dma((2, n_ba - 1)),
            dma((2, n_ba - 1)),
            dma((2, n_ba - 1)),
            dma((2, chips - 1)),
            dma((2, chips)),
            dma((2, n_ba - 1)),
        ],
        compiler_params=pltpu.CompilerParams(
            collective_id=0, has_side_effects=True, vmem_limit_bytes=48 * 1024 * 1024
        ),
    )(*operands)
    denoised, token_out = pl.pallas_call(
        finish_kernel,
        out_shape=[
            jax.ShapeDtypeStruct((3, atoms), F32),
            jax.ShapeDtypeStruct((tok_rows, width), F32),
        ],
        in_specs=[vmem, vmem],
        out_specs=[vmem, vmem],
        compiler_params=pltpu.CompilerParams(vmem_limit_bytes=8 * 1024 * 1024),
    )(tokens.reshape(tok_rows, width), denoised)
    return denoised, token_out


def solution(mesh):
    in_specs = (
        P(("aa", "ba"), None),
        P(None, ("aa", "ba")),
        P(),
        P(("aa", "ba")),
        P("aa", None),
        P("aa", "ba", None),
    ) + (P(),) * 11
    out_specs = (P(None, ("aa", "ba")), P("aa", None))
    return jax.shard_map(
        functools.partial(on_device, mesh.shape["aa"], mesh.shape["ba"]),
        mesh=mesh,
        in_specs=in_specs,
        out_specs=out_specs,
        check_vma=False,
    )
```

```python
import functools

import jax
import jax.numpy as jnp
from jax import lax
from jax.experimental import pallas as pl
from jax.experimental.pallas import tpu as pltpu
from jax.sharding import PartitionSpec as P

MESH = pl.DeviceIdType.MESH
F32 = jnp.float32
BF16 = jnp.bfloat16
LANES = 128
PAIR_CHUNKS = 4
EARLY_CHUNKS = 2
BIAS_ROWS = 8


def flip(index, mask):
    out = index
    bit = 1
    while bit <= mask:
        if mask & bit:
            out = out + bit - 2 * bit * lax.rem(index // bit, 2)
        bit *= 2
    return out


def far_first(count):
    return sorted(range(1, count), key=lambda m: (-bin(m).count("1"), m))


def norm(values, gain_row):
    mean_value = jnp.mean(values, axis=-1, keepdims=True)
    centered = values - mean_value
    variance = jnp.mean(centered * centered, axis=-1, keepdims=True)
    scaled = centered * lax.rsqrt(variance + 1e-05)
    return scaled if gain_row is None else scaled * gain_row


def dot(a, b):
    return jnp.dot(a, b, preferred_element_type=F32)


def dot_nt(a, b):
    return lax.dot_general(a, b, (((1,), (1,)), ((), ())), preferred_element_type=F32)


def step_kernel(
    n_aa,
    n_ba,
    atom_hbm,
    noisy_hbm,
    noise_ref,
    ids_hbm,
    tok_hbm,
    pair_hbm,
    bias_w_hbm,
    gains_hbm,
    w_pos_hbm,
    wat_hbm,
    wqg_hbm,
    wkv_hbm,
    wo_hbm,
    wup_hbm,
    wdn_hbm,
    wta_hbm,
    w_pos_out_hbm,
    den_ref,
    t_all,
    noisy_ref,
    bias_w_ref,
    gains_ref,
    w_pos_ref,
    w_pos_out_ref,
    v_state,
    v_post,
    v_onehot,
    v_tok,
    v_pair,
    v_bias,
    bias_send,
    v_wat,
    v_wqg,
    v_wkv,
    v_wod,
    v_wup,
    v_wta,
    v_ids,
    ids_mate,
    ids_all,
    state_own,
    state_mate,
    sum_send,
    sum_recv,
    rows_own,
    rows_kv,
    q_own,
    q_all,
    v_km,
    v_vm,
    v_p,
    o_send,
    o_recv,
    st_send,
    st_recv,
    v_inner,
    t_own,
    ta_own,
    ta_all,
    load_sem,
    pair_sem,
    ids_mate_sems,
    ids_sems,
    state_sems,
    sum_sems,
    bias_sems,
    kv_send,
    kv_recv,
    kv_local,
    kvm_sems,
    q_sems,
    o_sems,
    st_sems,
    t_sems,
    tm_sems,
    ta_sems,
):
    atoms = noisy_ref.shape[1]
    atoms_pad = v_state.shape[0]
    tok_rows, cols, channels = v_pair.shape
    heads = bias_w_ref.shape[0]
    half = heads // 2
    own, width = v_tok.shape
    head_dim = width // heads
    span = width // 2
    hidden = v_wod.shape[0] - width
    halves, half_rows = rows_own.shape[:2]
    chips = n_ba // 2
    keys_n = 2 * cols
    me_a = lax.axis_index("aa")
    me_b = lax.axis_index("ba")
    core = lax.rem(me_b, 2)
    chip = me_b // 2

    own_start = pl.multiple_of(me_b * own, own)
    span_start = pl.multiple_of(core * span, LANES)
    copies = [
        ("ids", ids_hbm, v_ids.at[0]),
        ("noisy", noisy_hbm, noisy_ref),
        ("atom", atom_hbm, v_state.at[pl.ds(0, atoms)]),
        ("w_pos", w_pos_hbm, w_pos_ref),
        ("wat", wat_hbm, v_wat),
        ("bias_w", bias_w_hbm, bias_w_ref),
        ("gains", gains_hbm, gains_ref),
        ("tok", tok_hbm.at[pl.ds(own_start, own)], v_tok),
        ("w_pos_out", w_pos_out_hbm, w_pos_out_ref),
        ("wqg", wqg_hbm, v_wqg),
        ("wkv", wkv_hbm.at[:, pl.ds(span_start, span)], v_wkv.at[:, pl.ds(0, span)]),
        (
            "wkv",
            wkv_hbm.at[:, pl.ds(pl.multiple_of(width + core * span, LANES), span)],
            v_wkv.at[:, pl.ds(span, span)],
        ),
        ("wod", wo_hbm, v_wod.at[pl.ds(0, width)]),
        ("wup", wup_hbm, v_wup),
        ("wod", wdn_hbm, v_wod.at[pl.ds(width, hidden)]),
        ("wta", wta_hbm, v_wta),
    ]
    names = list(dict.fromkeys(name for name, _, _ in copies))

    def load(name):
        for key, src, dst in copies:
            if key == name:
                pltpu.make_async_copy(src, dst, load_sem.at[names.index(name)]).start()

    def take(whole, sem):
        pltpu.make_async_copy(whole, whole, sem).wait()

    def loaded(name, whole):
        take(whole, load_sem.at[names.index(name)])

    step = tok_rows // PAIR_CHUNKS
    pair_loads = [
        pltpu.make_async_copy(
            pair_hbm.at[pl.ds(c * step, step)], v_pair.at[pl.ds(c * step, step)], pair_sem.at[c]
        )
        for c in range(PAIR_CHUNKS)
    ]
    for name in names[:5]:
        load(name)

    def at(a, b):
        return {"aa": a, "ba": b}

    def greet(device):
        pl.semaphore_signal(barrier, inc=1, device_id=device, device_id_type=MESH)

    barrier = pltpu.get_barrier_semaphore()
    for x in range(1, n_ba):
        greet(at(me_a, flip(me_b, x)))
    for x in range(1, n_aa):
        greet(at(flip(me_a, x), 2 * me_a + core))
    for x in range(1, chips):
        greet(at(chip, flip(me_b, 2 * x)))

    @pl.when(chip != me_a)
    def _():
        greet(at(me_a, 2 * me_a + core))
        greet(at(chip, me_b))

    greetings = n_ba - 1 + n_aa - 1 + chips - 1 + jnp.where(chip != me_a, 2, 0)

    for name in names[5:8]:
        load(name)
    for copy in pair_loads:
        copy.start()
    for name in names[8:]:
        load(name)
    if atoms_pad > atoms:
        v_state[pl.ds(atoms, atoms_pad - atoms), :] = jnp.zeros(
            (atoms_pad - atoms, channels), F32
        )

    def ba_copy(src, dst, sems, x, slot=1):
        return pltpu.make_async_remote_copy(
            src_ref=src,
            dst_ref=dst,
            send_sem=sems.at[0],
            recv_sem=sems.at[slot],
            device_id=at(me_a, flip(me_b, x)),
            device_id_type=MESH,
        )

    order = far_first(n_ba)
    chip_order = far_first(chips)

    loaded("noisy", noisy_ref)
    sigma = jnp.full((3, atoms), noise_ref[0], F32)
    inv_scale = 1.0 / jnp.sqrt(sigma * sigma + 1.0)
    v_post[...] = jnp.full(v_post.shape, -1.0, F32)
    v_post[0:3, 0:atoms] = noisy_ref[...] * inv_scale
    loaded("ids", v_ids.at[0])
    ids_row = v_ids[...]
    v_post[3:4, :] = ids_row.astype(F32)
    columns = v_post[...].T
    loaded("w_pos", w_pos_ref)
    loaded("atom", v_state.at[pl.ds(0, atoms)])
    state = v_state[...]
    for c in range(3):
        state = state + columns[:, c : c + 1] * w_pos_ref[c : c + 1, :]
    v_state[...] = state
    rounded = state.astype(BF16)
    state_own[...] = rounded

    pl.semaphore_wait(barrier, greetings)
    ba_copy(state_own, state_mate, state_sems, 1).start()
    ba_copy(v_ids, ids_mate, ids_mate_sems, 1).start()
    for x in order:
        ba_copy(v_ids, ids_all.at[x - 1], ids_sems, x).start()

    def select(ids, part):
        row = lax.broadcasted_iota(jnp.int32, (chips * half_rows, atoms_pad), 0)
        token = lax.rem(row, half_rows) + 2 * own * (row // half_rows)
        token = token + (own * core + me_a * tok_rows + part * half_rows)
        return jnp.where(token == ids, 1.0, 0.0).astype(BF16)

    loaded("wat", v_wat)
    hidden_own = jnp.maximum(dot(rounded, v_wat[...]), 0.0).astype(BF16)
    own_sums = [dot(select(ids_row, part), hidden_own) for part in range(halves)]
    take(ids_mate, ids_mate_sems.at[1])
    selectors = [select(ids_mate[...], part) for part in range(halves)]
    take(state_mate, state_sems.at[1])
    hidden_mate = jnp.maximum(dot(state_mate[...], v_wat[...]), 0.0).astype(BF16)
    for part in range(halves):
        chip_sums = own_sums[part] + dot(selectors[part], hidden_mate)
        sum_send[part] = chip_sums.astype(BF16).reshape(chips, half_rows, width)
        for d in chip_order:
            ba_copy(
                sum_send.at[part, flip(chip, d)],
                sum_recv.at[part, d - 1],
                sum_sems,
                2 * d,
                1 + part,
            ).start()

    lane_id = lax.broadcasted_iota(jnp.int32, (atoms_pad, tok_rows), 1) + me_a * tok_rows
    v_onehot[...] = jnp.where(columns[:, 3:4] == lane_id.astype(F32), 1.0, 0.0).astype(BF16)
    loaded("bias_w", bias_w_ref)
    weights_all = bias_w_ref[...].astype(F32)
    first_half, second_half = weights_all[0:half], weights_all[half:heads]
    bias_w = jnp.concatenate(
        [
            jnp.where(core == 0, first_half, second_half),
            jnp.where(core == 0, second_half, first_half),
        ],
        axis=0,
    ).astype(BF16)
    bias_rows = step * half
    bias_copies = [
        ba_copy(
            bias_send.at[pl.ds(c * bias_rows, bias_rows)],
            v_bias.at[core, pl.ds(c * bias_rows, bias_rows)],
            bias_sems,
            1,
        )
        for c in range(PAIR_CHUNKS)
    ]

    def bias_chunk(c):
        pair_loads[c].wait()

        def rows(r, carry):
            start = c * step + r * BIAS_ROWS
            block = v_pair[pl.ds(start, BIAS_ROWS)].reshape(BIAS_ROWS * cols, channels)
            out = dot_nt(bias_w, block)
            for i in range(BIAS_ROWS):
                where = pl.ds(pl.multiple_of((start + i) * half, half), half)
                v_bias[core, where, :] = out[0:half, i * cols : (i + 1) * cols]
                bias_send[where, :] = out[half:heads, i * cols : (i + 1) * cols]
            return carry

        lax.fori_loop(0, step // BIAS_ROWS, rows, 0)
        bias_copies[c].start()

    for c in range(EARLY_CHUNKS):
        bias_chunk(c)

    own_row = lax.broadcasted_iota(jnp.int32, (own, atoms_pad), 0) + (
        me_a * tok_rows + me_b * own
    )
    take(ids_all, ids_sems.at[1])
    hits = jnp.where(own_row == ids_row, 1.0, 0.0)
    for x in order:
        hits = hits + jnp.where(own_row == ids_all[x - 1], 1.0, 0.0)
    counts = jnp.sum(hits, axis=1, keepdims=True)
    loaded("tok", v_tok)
    loaded("gains", gains_ref)

    def kv_copy(x, part):
        return pltpu.make_async_remote_copy(
            src_ref=rows_own.at[part],
            dst_ref=rows_kv.at[me_b, part],
            send_sem=kv_send.at[1 if x else 0],
            recv_sem=kv_recv.at[part, chip],
            device_id=at(flip(me_a, x), 2 * me_a + core),
            device_id_type=MESH,
        )

    own_piece = pltpu.make_async_copy(rows_own, rows_kv.at[me_b], kv_local)
    for part in range(halves):
        rows = pl.ds(part * half_rows, half_rows)
        summed = sum_send[part, chip].astype(F32)
        take(sum_recv.at[part], sum_sems.at[1 + part])
        for d in chip_order:
            summed = summed + sum_recv[part, d - 1].astype(F32)
        tokens_start = (
            v_tok[rows, :] + summed / counts[part * half_rows : (part + 1) * half_rows]
        )
        v_tok[rows, :] = tokens_start
        rows_own[part] = norm(tokens_start, gains_ref[0:1, :]).astype(BF16)
        for x in far_first(n_aa):
            kv_copy(x, part).start()

        @pl.when(chip != me_a)
        def _():
            kv_copy(0, part).start()

    @pl.when(chip == me_a)
    def _():
        own_piece.start()

    normed = rows_own[...].reshape(own, width)
    loaded("wqg", v_wqg)
    query = dot(normed, v_wqg[:, 0:width]).astype(BF16)
    for c in range(2):
        q_own[c] = query[:, c * span : (c + 1) * span]
    q_all[me_b] = q_own[core]
    for x in order:
        ba_copy(q_own.at[lax.rem(core + x, 2)], q_all.at[me_b], q_sems, x).start()
    gate = jax.nn.sigmoid(dot(normed, v_wqg[:, width : 2 * width])).astype(BF16)

    for c in range(EARLY_CHUNKS, PAIR_CHUNKS):
        bias_chunk(c)

    @pl.when(chip == me_a)
    def _():
        own_piece.wait()

    for part in range(halves):
        for d in range(chips):
            piece = flip(me_b, 2 * d)
            rows = rows_kv.at[piece, part]
            arrival = kv_recv.at[part, flip(chip, d)]
            if d:
                take(rows, arrival)
            else:

                @pl.when(chip != me_a)
                def _():
                    take(rows, arrival)

            ba_copy(rows, rows, kvm_sems, 1).start()
    loaded("wkv", v_wkv)
    chip_pieces = rows_kv.at[pl.ds(0, chips)]
    take(chip_pieces, kvm_sems.at[1])

    key_value = dot(rows_kv[...].reshape(keys_n, width), v_wkv[...])
    spans = []
    for h in range(half):
        lo = h * head_dim // LANES * LANES
        hi = ((h + 1) * head_dim + LANES - 1) // LANES * LANES
        spans.append((lo, hi))
        lane = lax.broadcasted_iota(jnp.int32, (keys_n, hi - lo), 1) + lo
        mine = (lane >= h * head_dim) & (lane < (h + 1) * head_dim)
        v_km[h, :, 0 : hi - lo] = jnp.where(mine, key_value[:, lo:hi], 0.0).astype(BF16)
    tiles = []
    for t in range(span // LANES):
        h0 = t * LANES // head_dim
        h1 = (t * LANES + LANES - 1) // head_dim
        tiles.append((h0, h1))
        part = key_value[:, span + t * LANES : span + (t + 1) * LANES]
        lane = lax.broadcasted_iota(jnp.int32, (keys_n, LANES), 1) + t * LANES
        for h in range(h0, h1 + 1):
            mine = (lane >= h * head_dim) & (lane < (h + 1) * head_dim)
            v_vm[t, (h - h0) * keys_n : (h - h0 + 1) * keys_n, :] = jnp.where(
                mine, part, 0.0
            ).astype(BF16)

    q_pieces = q_all.at[pl.ds(0, n_ba - 1)]
    take(q_pieces, q_sems.at[1])
    take(bias_send, bias_sems.at[1])

    scale = head_dim ** (-0.5)
    rows2 = 2 * own
    lane = lax.broadcasted_iota(jnp.int32, (rows2, LANES), 1)
    top_lane = lane - half * core
    groups = own // 8
    for d in chip_order + [0]:
        duo = flip(chip, d)
        stats = jnp.zeros((rows2, LANES), F32)
        q_rows = q_all[pl.ds(2 * duo, 2)].reshape(rows2, span)
        for h in range(half):
            lo, hi = spans[h]
            scores = dot_nt(q_rows[:, lo:hi], v_km[h, :, 0 : hi - lo]) * scale
            where = pl.ds(duo * (rows2 * half) + h, rows2, stride=half)
            parts = [
                scores[:, k * cols : (k + 1) * cols] + v_bias[k, where, :] for k in range(2)
            ]
            top = jnp.max(jnp.maximum(parts[0], parts[1]), axis=1, keepdims=True)
            parts = [jnp.exp(part - top) for part in parts]
            total = jnp.sum(parts[0] + parts[1], axis=1, keepdims=True)
            stats = jnp.where(top_lane == h, top, stats)
            stats = jnp.where(top_lane == heads + h, total, stats)
            for k in range(2):
                v_p[:, h * keys_n + k * cols : h * keys_n + (k + 1) * cols] = parts[k].astype(
                    BF16
                )
        for t, (h0, h1) in enumerate(tiles):
            out = dot(
                v_p[:, h0 * keys_n : (h1 + 1) * keys_n], v_vm[t, 0 : (h1 - h0 + 1) * keys_n, :]
            )
            o_send[pl.ds(2 * duo, 2), :, t * LANES : (t + 1) * LANES] = out.astype(BF16).reshape(
                2, own, LANES
            )
        for c in range(2):
            packed = stats[c * own : c * own + 8]
            for g in range(1, groups):
                piece = pltpu.roll(stats[c * own + 8 * g : c * own + 8 * g + 8], 2 * heads * g, 1)
                packed = jnp.where(lane[0:8] >= 2 * heads * g, piece, packed)
            st_send[2 * duo + c] = packed
        for x in (2 * d + 1, 2 * d):
            if x:
                target = flip(me_b, x)
                ba_copy(st_send.at[target], st_recv.at[x - 1], st_sems, x).start()
                ba_copy(o_send.at[target], o_recv.at[x - 1], o_sems, x).start()

    def unpack(packed):
        parts = [packed]
        for g in range(1, groups):
            parts.append(pltpu.roll(packed, LANES - 2 * heads * g, 1))
        return jnp.concatenate(parts, axis=0)

    take(st_recv, st_sems.at[1])
    tops = []
    for d in range(chips):
        mine = st_recv[2 * d - 1] if d else st_send[me_b]
        tops.append(unpack(mine + st_recv[2 * d]))
    overall = tops[0]
    for top in tops[1:]:
        overall = jnp.maximum(overall, top)
    factors = [jnp.exp(top - overall) for top in tops]
    denominator = jnp.zeros((own, LANES), F32)
    for factor, top in zip(factors, tops):
        denominator = denominator + factor * pltpu.roll(top, LANES - heads, 1)
    head_row = lax.broadcasted_iota(jnp.int32, (LANES, width), 0)
    head_lane = lax.broadcasted_iota(jnp.int32, (LANES, width), 1)
    inside = (head_lane >= head_row * head_dim) & (head_lane < (head_row + 1) * head_dim)
    spread = jnp.where(inside, 1.0, 0.0).astype(BF16)
    live = lane[0:own] < heads
    shares = jnp.concatenate(
        [jnp.where(live, factor / denominator, 0.0) for factor in factors], axis=0
    )
    coarse = shares.astype(BF16)
    fine = (shares - coarse.astype(F32)).astype(BF16)
    wide = dot(coarse, spread) + dot(fine, spread)
    take(o_recv, o_sems.at[1])
    left = jnp.zeros((own, span), F32)
    right = jnp.zeros((own, span), F32)
    for d in range(chips):
        mine = (o_recv[2 * d - 1] if d else o_send[me_b]).astype(F32)
        other = o_recv[2 * d].astype(F32)
        part = wide[d * own : (d + 1) * own]
        left = left + part[:, 0:span] * jnp.where(core == 0, mine, other)
        right = right + part[:, span:width] * jnp.where(core == 0, other, mine)
    attended = jnp.concatenate([left, right], axis=1)
    mixed = (attended * gate.astype(F32)).astype(BF16)
    loaded("wod", v_wod)
    tokens_mid = v_tok[...] + dot(mixed, v_wod[0:width, :])
    normed_mid = norm(tokens_mid, gains_ref[1:2, :]).astype(BF16)
    loaded("wup", v_wup)
    part = 512
    for n in range(0, hidden, part):
        first = dot(normed_mid, v_wup[:, n : n + part])
        second = dot(normed_mid, v_wup[:, hidden + n : hidden + n + part])
        v_inner[:, n : n + part] = (first * jax.nn.sigmoid(first) * second).astype(BF16)
    outs = []
    for c in range(2):
        columns_c = pl.ds(c * span, span)
        out = dot(v_inner[...], v_wod[width : width + hidden, c * span : (c + 1) * span])
        out = tokens_mid[:, c * span : (c + 1) * span] + out
        outs.append(out)
        t_own[:, columns_c] = out.astype(BF16)
        t_all[me_b, :, columns_c] = out.astype(BF16)
        for d in chip_order:
            ba_copy(
                t_own.at[:, columns_c], t_all.at[me_b, :, columns_c], t_sems, 2 * d, d
            ).start()
    token_out = jnp.concatenate(outs, axis=1)
    ba_copy(t_own, t_all.at[me_b], tm_sems, 1).start()
    loaded("wta", v_wta)
    normed_out = norm(token_out, gains_ref[2:3, :]).astype(BF16)
    token_atom = dot(normed_out, v_wta[...]).astype(BF16)
    ta_own[...] = token_atom
    ta_all[me_b] = token_atom
    for x in order:
        ba_copy(ta_own, ta_all.at[me_b], ta_sems, x).start()
    loaded("w_pos_out", w_pos_out_ref)
    for d in range(1, chips):
        rows = t_all.at[flip(me_b, 2 * d)]
        take(rows, t_sems.at[d])
        ba_copy(rows, rows, tm_sems, 1).start()
    ta_pieces = ta_all.at[pl.ds(0, n_ba - 1)]
    take(ta_pieces, ta_sems.at[1])
    picked = dot(v_onehot[...], ta_all[...].reshape(tok_rows, channels))
    atom_normed = norm(v_state[...] + picked, None).astype(BF16)
    update = dot_nt(w_pos_out_ref[...], atom_normed)[:, 0:atoms]
    den_ref[...] = noisy_ref[...] * (inv_scale * inv_scale) + update * (sigma * inv_scale)
    t_pieces = t_all.at[pl.ds(0, chips)]
    take(t_pieces, tm_sems.at[1])
    for whole, sem in (
        (state_mate, state_sems),
        (ids_mate, ids_mate_sems),
        (ids_all, ids_sems),
        (sum_recv, sum_sems),
        (bias_send, bias_sems),
        (chip_pieces, kvm_sems),
        (q_pieces, q_sems),
        (st_recv, st_sems),
        (o_recv, o_sems),
        (t_all.at[pl.ds(0, chips - 1)], t_sems),
        (t_pieces, tm_sems),
        (ta_pieces, ta_sems),
    ):
        take(whole, sem.at[0])
    take(rows_kv.at[pl.ds(0, n_aa - 1)], kv_send.at[1])

    @pl.when(chip != me_a)
    def _():
        take(rows_own, kv_send.at[0])


def finish_kernel(tok_ref, den_ref, den_out_ref, tok_out_ref):
    den_out_ref[...] = den_ref[...]
    tok_out_ref[...] = tok_ref[...].astype(F32)


def on_device(
    n_aa,
    n_ba,
    atom_cond,
    noisy_pos,
    noise_level,
    atom_token,
    token_cond,
    pair,
    pair_bias_weight,
    gains,
    w_pos,
    w_atom_token,
    w_query_gate,
    w_key_value,
    w_attn_out,
    w_up,
    w_down,
    w_token_atom,
    w_pos_out,
):
    atoms, channels = atom_cond.shape
    atoms_pad = -(-atoms // LANES) * LANES
    tok_rows, width = token_cond.shape
    cols = pair.shape[1]
    heads = pair_bias_weight.shape[0]
    own = tok_rows // n_ba
    chips = n_ba // 2
    half, span, keys_n = heads // 2, width // 2, 2 * cols
    halves = 2 if own % 32 == 0 else 1
    half_rows = own // halves
    head_dim = width // heads
    if tok_rows != 2 * cols or chips != n_aa:
        raise ValueError("unsupported mesh")
    tile_heads = max(
        (t * LANES + LANES - 1) // head_dim - t * LANES // head_dim + 1
        for t in range(span // LANES)
    )
    ids = atom_token
    if atoms_pad > atoms:
        ids = jnp.pad(atom_token, (0, atoms_pad - atoms), constant_values=-1)
    vmem = pl.BlockSpec(memory_space=pltpu.VMEM)
    smem = pl.BlockSpec(memory_space=pltpu.SMEM)
    hbm = pl.BlockSpec(memory_space=pltpu.HBM)
    dma = pltpu.SemaphoreType.DMA
    operands = [
        pltpu.with_memory_space_constraint(value, pltpu.HBM) if value.size > 1 else value
        for value in (
            atom_cond,
            noisy_pos,
            noise_level,
            ids,
            token_cond,
            pair,
            pair_bias_weight,
            gains,
            w_pos,
            w_atom_token,
            w_query_gate,
            w_key_value,
            w_attn_out,
            w_up,
            w_down,
            w_token_atom,
            w_pos_out,
        )
    ]
    denoised, tokens = pl.pallas_call(
        functools.partial(step_kernel, n_aa, n_ba),
        out_shape=[
            jax.ShapeDtypeStruct((3, atoms), F32),
            jax.ShapeDtypeStruct((n_ba, own, width), BF16),
        ],
        in_specs=[hbm, hbm, smem] + [hbm] * 14,
        out_specs=[vmem, vmem],
        scratch_shapes=[
            pltpu.VMEM((3, atoms), F32),
            pltpu.VMEM(pair_bias_weight.shape, BF16),
            pltpu.VMEM(gains.shape, F32),
            pltpu.VMEM(w_pos.shape, F32),
            pltpu.VMEM(w_pos_out.shape, BF16),
            pltpu.VMEM((atoms_pad, channels), F32),
            pltpu.VMEM((LANES, atoms_pad), F32),
            pltpu.VMEM((atoms_pad, tok_rows), BF16),
            pltpu.VMEM((own, width), F32),
            pltpu.VMEM(pair.shape, BF16),
            pltpu.VMEM((2, tok_rows * half, cols), F32),
            pltpu.VMEM((tok_rows * half, cols), F32),
            pltpu.VMEM(w_atom_token.shape, BF16),
            pltpu.VMEM(w_query_gate.shape, BF16),
            pltpu.VMEM((width, width), BF16),
            pltpu.VMEM((width + w_down.shape[0], width), BF16),
            pltpu.VMEM(w_up.shape, BF16),
            pltpu.VMEM(w_token_atom.shape, BF16),
            pltpu.VMEM((1, atoms_pad), jnp.int32),
            pltpu.VMEM((1, atoms_pad), jnp.int32),
            pltpu.VMEM((n_ba - 1, 1, atoms_pad), jnp.int32),
            pltpu.VMEM((atoms_pad, channels), BF16),
            pltpu.VMEM((atoms_pad, channels), BF16),
            pltpu.VMEM((halves, chips, half_rows, width), BF16),
            pltpu.VMEM((halves, chips - 1, half_rows, width), BF16),
            pltpu.VMEM((halves, half_rows, width), BF16),
            pltpu.VMEM((n_ba, halves, half_rows, width), BF16),
            pltpu.VMEM((2, own, span), BF16),
            pltpu.VMEM((n_ba, own, span), BF16),
            pltpu.VMEM((half, keys_n, 2 * LANES), BF16),
            pltpu.VMEM((span // LANES, tile_heads * keys_n, LANES), BF16),
            pltpu.VMEM((2 * own, half * keys_n), BF16),
            pltpu.VMEM((n_ba, own, span), BF16),
            pltpu.VMEM((n_ba - 1, own, span), BF16),
            pltpu.VMEM((n_ba, 8, LANES), F32),
            pltpu.VMEM((n_ba - 1, 8, LANES), F32),
            pltpu.VMEM((own, w_down.shape[0]), BF16),
            pltpu.VMEM((own, width), BF16),
            pltpu.VMEM((own, channels), BF16),
            pltpu.VMEM((n_ba, own, channels), BF16),
            dma((14,)),
            dma((PAIR_CHUNKS,)),
            dma((2,)),
            dma((2,)),
            dma((2,)),
            dma((1 + halves,)),
            dma((2,)),
            dma((2,)),
            dma((halves, chips)),
            dma,
            dma((2,)),
            dma((2,)),
            dma((2,)),
            dma((2,)),
            dma((chips,)),
            dma((2,)),
            dma((2,)),
        ],
        compiler_params=pltpu.CompilerParams(
            collective_id=0, has_side_effects=True, vmem_limit_bytes=48 * 1024 * 1024
        ),
    )(*operands)
    denoised, token_out = pl.pallas_call(
        finish_kernel,
        out_shape=[
            jax.ShapeDtypeStruct((3, atoms), F32),
            jax.ShapeDtypeStruct((tok_rows, width), F32),
        ],
        in_specs=[vmem, vmem],
        out_specs=[vmem, vmem],
        compiler_params=pltpu.CompilerParams(vmem_limit_bytes=8 * 1024 * 1024),
    )(tokens.reshape(tok_rows, width), denoised)
    return denoised, token_out


def solution(mesh):
    in_specs = (
        P(("aa", "ba"), None),
        P(None, ("aa", "ba")),
        P(),
        P(("aa", "ba")),
        P("aa", None),
        P("aa", "ba", None),
    ) + (P(),) * 11
    out_specs = (P(None, ("aa", "ba")), P("aa", None))
    return jax.shard_map(
        functools.partial(on_device, mesh.shape["aa"], mesh.shape["ba"]),
        mesh=mesh,
        in_specs=in_specs,
        out_specs=out_specs,
        check_vma=False,
    )
```

```python
import functools

import jax
import jax.numpy as jnp
from jax import lax
from jax.experimental import pallas as pl
from jax.experimental.pallas import tpu as pltpu
from jax.sharding import PartitionSpec as P

MESH = pl.DeviceIdType.MESH
F32 = jnp.float32
BF16 = jnp.bfloat16
LANES = 128
PAIR_CHUNKS = 8
EARLY_CHUNKS = 3
BIAS_ROWS = 8


def flip(index, mask):
    out = index
    bit = 1
    while bit <= mask:
        if mask & bit:
            out = out + bit - 2 * bit * lax.rem(index // bit, 2)
        bit *= 2
    return out


def far_first(count):
    return sorted(range(1, count), key=lambda m: (-bin(m).count("1"), m))


def norm(values, gain_row):
    mean_value = jnp.mean(values, axis=-1, keepdims=True)
    centered = values - mean_value
    variance = jnp.mean(centered * centered, axis=-1, keepdims=True)
    scaled = centered * lax.rsqrt(variance + 1e-05)
    return scaled if gain_row is None else scaled * gain_row


def dot(a, b):
    return jnp.dot(a, b, preferred_element_type=F32)


def dot_nt(a, b):
    return lax.dot_general(a, b, (((1,), (1,)), ((), ())), preferred_element_type=F32)


def step_kernel(
    n_aa,
    n_ba,
    atom_hbm,
    noisy_hbm,
    noise_ref,
    ids_hbm,
    tok_hbm,
    pair_hbm,
    bias_w_hbm,
    gains_hbm,
    w_pos_hbm,
    wat_hbm,
    wqg_hbm,
    wkv_hbm,
    wo_hbm,
    wup_hbm,
    wdn_hbm,
    wta_hbm,
    w_pos_out_hbm,
    den_ref,
    t_all,
    noisy_ref,
    bias_w_ref,
    gains_ref,
    w_pos_ref,
    w_pos_out_ref,
    v_state,
    v_post,
    v_onehot,
    v_tok,
    v_pair,
    v_bias,
    bias_send,
    v_wat,
    v_wqg,
    v_wkv,
    v_wod,
    v_wup,
    v_wta,
    v_ids,
    ids_mate,
    ids_all,
    state_own,
    state_mate,
    sum_send,
    sum_recv,
    rows_own,
    rows_kv,
    q_own,
    q_all,
    v_km,
    v_vm,
    v_p,
    o_send,
    o_recv,
    st_send,
    st_recv,
    v_inner,
    t_own,
    ta_own,
    ta_all,
    load_sem,
    pair_sem,
    ids_mate_sems,
    ids_sems,
    state_sems,
    sum_sems,
    bias_sems,
    kv_send,
    kv_recv,
    kvm_sems,
    q_sems,
    o_sems,
    st_sems,
    t_sems,
    tm_sems,
    ta_sems,
):
    atoms = noisy_ref.shape[1]
    atoms_pad = v_state.shape[0]
    tok_rows, cols, channels = v_pair.shape
    heads = bias_w_ref.shape[0]
    half = heads // 2
    own, width = v_tok.shape
    head_dim = width // heads
    span = width // 2
    hidden = v_wod.shape[0] - width
    parts, part_rows = rows_own.shape[:2]
    chips = n_ba // 2
    keys_n = 2 * cols
    me_a = lax.axis_index("aa")
    me_b = lax.axis_index("ba")
    core = lax.rem(me_b, 2)
    chip = me_b // 2

    own_start = pl.multiple_of(me_b * own, own)
    span_start = pl.multiple_of(core * span, LANES)
    copies = [
        ("ids", ids_hbm, v_ids.at[0]),
        ("noisy", noisy_hbm, noisy_ref),
        ("atom", atom_hbm, v_state.at[pl.ds(0, atoms)]),
        ("w_pos", w_pos_hbm, w_pos_ref),
        ("wat", wat_hbm, v_wat),
        ("bias_w", bias_w_hbm, bias_w_ref),
        ("gains", gains_hbm, gains_ref),
        ("tok", tok_hbm.at[pl.ds(own_start, own)], v_tok),
        ("w_pos_out", w_pos_out_hbm, w_pos_out_ref),
        ("wqg", wqg_hbm, v_wqg),
        ("wkv", wkv_hbm.at[:, pl.ds(span_start, span)], v_wkv.at[:, pl.ds(0, span)]),
        (
            "wkv",
            wkv_hbm.at[:, pl.ds(pl.multiple_of(width + core * span, LANES), span)],
            v_wkv.at[:, pl.ds(span, span)],
        ),
        ("wod", wo_hbm, v_wod.at[pl.ds(0, width)]),
        ("wup", wup_hbm, v_wup),
        ("wod", wdn_hbm, v_wod.at[pl.ds(width, hidden)]),
        ("wta", wta_hbm, v_wta),
    ]
    names = list(dict.fromkeys(name for name, _, _ in copies))

    def load(name):
        for key, src, dst in copies:
            if key == name:
                pltpu.make_async_copy(src, dst, load_sem.at[names.index(name)]).start()

    def take(whole, sem):
        pltpu.make_async_copy(whole, whole, sem).wait()

    def loaded(name, whole):
        take(whole, load_sem.at[names.index(name)])

    step = tok_rows // PAIR_CHUNKS
    pair_loads = [
        pltpu.make_async_copy(
            pair_hbm.at[pl.ds(c * step, step)], v_pair.at[pl.ds(c * step, step)], pair_sem.at[c]
        )
        for c in range(PAIR_CHUNKS)
    ]
    for name in names[:5]:
        load(name)

    def at(a, b):
        return {"aa": a, "ba": b}

    def greet(device):
        pl.semaphore_signal(barrier, inc=1, device_id=device, device_id_type=MESH)

    barrier = pltpu.get_barrier_semaphore()
    for x in range(1, n_ba):
        greet(at(me_a, flip(me_b, x)))
    block = me_b // chips
    column = 2 * me_a + block
    for x in range(1, n_aa):
        greet(at(flip(me_a, x), column))

    @pl.when(chip != me_a)
    def _():
        for j in range(chips):
            greet(at(chip, core * chips + j))

    greetings = n_ba - 1 + n_aa - 1 + jnp.where(chip != me_a, chips, 0)

    for name in names[5:8]:
        load(name)
    for copy in pair_loads:
        copy.start()
    for name in names[8:]:
        load(name)
    if atoms_pad > atoms:
        v_state[pl.ds(atoms, atoms_pad - atoms), :] = jnp.zeros(
            (atoms_pad - atoms, channels), F32
        )

    def ba_copy(src, dst, sems, x, slot=1):
        return pltpu.make_async_remote_copy(
            src_ref=src,
            dst_ref=dst,
            send_sem=sems.at[0],
            recv_sem=sems.at[slot],
            device_id=at(me_a, flip(me_b, x)),
            device_id_type=MESH,
        )

    order = far_first(n_ba)
    chip_order = far_first(chips)

    loaded("noisy", noisy_ref)
    sigma = jnp.full((3, atoms), noise_ref[0], F32)
    inv_scale = 1.0 / jnp.sqrt(sigma * sigma + 1.0)
    v_post[...] = jnp.full(v_post.shape, -1.0, F32)
    v_post[0:3, 0:atoms] = noisy_ref[...] * inv_scale
    loaded("ids", v_ids.at[0])
    ids_row = v_ids[...]
    v_post[3:4, :] = ids_row.astype(F32)
    columns = v_post[...].T
    loaded("w_pos", w_pos_ref)
    loaded("atom", v_state.at[pl.ds(0, atoms)])
    state = v_state[...]
    for c in range(3):
        state = state + columns[:, c : c + 1] * w_pos_ref[c : c + 1, :]
    v_state[...] = state
    rounded = state.astype(BF16)
    state_own[...] = rounded

    pl.semaphore_wait(barrier, greetings)
    ba_copy(state_own, state_mate, state_sems, 1).start()
    ba_copy(v_ids, ids_mate, ids_mate_sems, 1).start()
    for x in order:
        ba_copy(v_ids, ids_all.at[x - 1], ids_sems, x).start()

    group = max(1, parts // 2)

    def select(ids, first):
        row = lax.broadcasted_iota(jnp.int32, (group * chips * part_rows, atoms_pad), 0)
        token = lax.rem(row, part_rows) + 2 * own * lax.rem(row // part_rows, chips)
        token = token + part_rows * (first + row // (part_rows * chips))
        token = token + (own * core + me_a * tok_rows)
        return jnp.where(token == ids, 1.0, 0.0).astype(BF16)

    loaded("wat", v_wat)
    hidden_own = jnp.maximum(dot(rounded, v_wat[...]), 0.0).astype(BF16)
    firsts = range(0, parts, group)
    own_sums = [dot(select(ids_row, first), hidden_own) for first in firsts]
    take(ids_mate, ids_mate_sems.at[1])
    selectors = [select(ids_mate[...], first) for first in firsts]
    take(state_mate, state_sems.at[1])
    hidden_mate = jnp.maximum(dot(state_mate[...], v_wat[...]), 0.0).astype(BF16)
    for first, sums, selector in zip(firsts, own_sums, selectors):
        chip_sums = sums + dot(selector, hidden_mate)
        sum_send[first : first + group] = chip_sums.astype(BF16).reshape(
            group, chips, part_rows, width
        )
        for part in range(first, first + group):
            for d in chip_order:
                ba_copy(
                    sum_send.at[part, flip(chip, d)],
                    sum_recv.at[part, d - 1],
                    sum_sems,
                    2 * d,
                    1 + part,
                ).start()

    lane_id = lax.broadcasted_iota(jnp.int32, (atoms_pad, tok_rows), 1) + me_a * tok_rows
    v_onehot[...] = jnp.where(columns[:, 3:4] == lane_id.astype(F32), 1.0, 0.0).astype(BF16)
    loaded("bias_w", bias_w_ref)
    weights_all = bias_w_ref[...].astype(F32)
    first_half, second_half = weights_all[0:half], weights_all[half:heads]
    bias_w = jnp.concatenate(
        [
            jnp.where(core == 0, first_half, second_half),
            jnp.where(core == 0, second_half, first_half),
        ],
        axis=0,
    ).astype(BF16)
    bias_rows = step * half
    bias_copies = [
        ba_copy(
            bias_send.at[pl.ds(c * bias_rows, bias_rows)],
            v_bias.at[core, pl.ds(c * bias_rows, bias_rows)],
            bias_sems,
            1,
        )
        for c in range(PAIR_CHUNKS)
    ]

    def bias_chunk(c):
        pair_loads[c].wait()

        def rows(r, carry):
            start = c * step + r * BIAS_ROWS
            block = v_pair[pl.ds(start, BIAS_ROWS)].reshape(BIAS_ROWS * cols, channels)
            out = dot_nt(bias_w, block)
            for i in range(BIAS_ROWS):
                where = pl.ds(pl.multiple_of((start + i) * half, half), half)
                v_bias[core, where, :] = out[0:half, i * cols : (i + 1) * cols]
                bias_send[where, :] = out[half:heads, i * cols : (i + 1) * cols]
            return carry

        lax.fori_loop(0, step // BIAS_ROWS, rows, 0)
        bias_copies[c].start()

    for c in range(EARLY_CHUNKS):
        bias_chunk(c)

    own_row = lax.broadcasted_iota(jnp.int32, (own, atoms_pad), 0) + (
        me_a * tok_rows + me_b * own
    )
    take(ids_all, ids_sems.at[1])
    hits = jnp.where(own_row == ids_row, 1.0, 0.0)
    for x in order:
        hits = hits + jnp.where(own_row == ids_all[x - 1], 1.0, 0.0)
    counts = jnp.sum(hits, axis=1, keepdims=True)
    loaded("tok", v_tok)
    loaded("gains", gains_ref)

    slot = lax.rem(me_b, chips)

    def kv_copy(x, part):
        return pltpu.make_async_remote_copy(
            src_ref=rows_own.at[part],
            dst_ref=rows_kv.at[me_b, part],
            send_sem=kv_send.at[1 if x else 0],
            recv_sem=kv_recv.at[part, slot],
            device_id=at(flip(me_a, x), column),
            device_id_type=MESH,
        )

    for part in range(parts):
        rows = pl.ds(part * part_rows, part_rows)
        summed = sum_send[part, chip].astype(F32)
        take(sum_recv.at[part], sum_sems.at[1 + part])
        for d in chip_order:
            summed = summed + sum_recv[part, d - 1].astype(F32)
        tokens_start = (
            v_tok[rows, :] + summed / counts[part * part_rows : (part + 1) * part_rows]
        )
        v_tok[rows, :] = tokens_start
        rows_own[part] = norm(tokens_start, gains_ref[0:1, :]).astype(BF16)
        for x in range(n_aa - 1, 0, -1):
            kv_copy(x, part).start()

        @pl.when(column != me_b)
        def _():
            kv_copy(0, part).start()

        @pl.when(column == me_b)
        def _():
            pltpu.make_async_copy(
                rows_own.at[part], rows_kv.at[me_b, part], kv_recv.at[part, slot]
            ).start()

    normed = rows_own[...].reshape(own, width)
    loaded("wqg", v_wqg)
    query = dot(normed, v_wqg[:, 0:width]).astype(BF16)
    for c in range(2):
        q_own[c] = query[:, c * span : (c + 1) * span]
    q_all[me_b] = q_own[core]
    for x in order:
        ba_copy(q_own.at[lax.rem(core + x, 2)], q_all.at[me_b], q_sems, x).start()
    gate = jax.nn.sigmoid(dot(normed, v_wqg[:, width : 2 * width])).astype(BF16)

    for c in range(EARLY_CHUNKS, PAIR_CHUNKS):
        bias_chunk(c)
    for part in range(parts):
        for j in range(chips):
            rows = rows_kv.at[core * chips + j, part]
            take(rows, kv_recv.at[part, j])
            ba_copy(rows, rows, kvm_sems, 1).start()
    loaded("wkv", v_wkv)
    chip_pieces = rows_kv.at[pl.ds(0, chips)]
    spans = []
    for h in range(half):
        lo = h * head_dim // LANES * LANES
        hi = ((h + 1) * head_dim + LANES - 1) // LANES * LANES
        spans.append((lo, hi))
    tiles = []
    for t in range(span // LANES):
        tiles.append((t * LANES // head_dim, (t * LANES + LANES - 1) // head_dim))

    def project(which):
        pieces = rows_kv[pl.ds(which * chips, chips)].reshape(cols, width)
        key_value = dot(pieces, v_wkv[...])
        keys = pl.ds(pl.multiple_of(which * cols, cols), cols)
        for h, (lo, hi) in enumerate(spans):
            lane = lax.broadcasted_iota(jnp.int32, (cols, hi - lo), 1) + lo
            mine = (lane >= h * head_dim) & (lane < (h + 1) * head_dim)
            v_km[h, keys, 0 : hi - lo] = jnp.where(mine, key_value[:, lo:hi], 0.0).astype(BF16)
        for t, (h0, h1) in enumerate(tiles):
            piece = key_value[:, span + t * LANES : span + (t + 1) * LANES]
            lane = lax.broadcasted_iota(jnp.int32, (cols, LANES), 1) + t * LANES
            for h in range(h0, h1 + 1):
                mine = (lane >= h * head_dim) & (lane < (h + 1) * head_dim)
                v_vm[t, h - h0, keys, :] = jnp.where(mine, piece, 0.0).astype(BF16)

    project(core)
    take(chip_pieces, kvm_sems.at[1])
    project(1 - core)

    q_pieces = q_all.at[pl.ds(0, n_ba - 1)]
    take(q_pieces, q_sems.at[1])
    take(bias_send, bias_sems.at[1])

    scale = head_dim ** (-0.5)
    rows2 = 2 * own
    batches = [chip_order[:2]] + [[d] for d in chip_order[2:]] + [[0]]
    groups = own // 8
    for duos in batches:
        places = [flip(chip, d) for d in duos]
        many = len(places)
        lane = lax.broadcasted_iota(jnp.int32, (many * rows2, LANES), 1)
        top_lane = lane - half * core
        stats = jnp.zeros((many * rows2, LANES), F32)
        q_rows = jnp.concatenate(
            [q_all[pl.ds(2 * duo, 2)].reshape(rows2, span) for duo in places], axis=0
        )
        for h in range(half):
            lo, hi = spans[h]
            scores = dot_nt(q_rows[:, lo:hi], v_km[h, :, 0 : hi - lo]) * scale
            pair_bias = [
                jnp.concatenate(
                    [
                        v_bias[k, pl.ds(duo * (rows2 * half) + h, rows2, stride=half), :]
                        for duo in places
                    ],
                    axis=0,
                )
                for k in range(2)
            ]
            both = [scores[:, k * cols : (k + 1) * cols] + pair_bias[k] for k in range(2)]
            top = jnp.max(jnp.maximum(both[0], both[1]), axis=1, keepdims=True)
            both = [jnp.exp(one - top) for one in both]
            total = jnp.sum(both[0] + both[1], axis=1, keepdims=True)
            stats = jnp.where(top_lane == h, top, stats)
            stats = jnp.where(top_lane == heads + h, total, stats)
            for k in range(2):
                v_p[0 : many * rows2, h * keys_n + k * cols : h * keys_n + (k + 1) * cols] = both[k].astype(BF16)
        for t, (h0, h1) in enumerate(tiles):
            count = (h1 - h0 + 1) * keys_n
            out = dot(
                v_p[0 : many * rows2, h0 * keys_n : h0 * keys_n + count],
                v_vm[t, 0 : h1 - h0 + 1].reshape(count, LANES),
            ).astype(BF16)
            for i, duo in enumerate(places):
                o_send[pl.ds(2 * duo, 2), :, t * LANES : (t + 1) * LANES] = out[
                    i * rows2 : (i + 1) * rows2
                ].reshape(2, own, LANES)
        for i, duo in enumerate(places):
            for c in range(2):
                at_row = i * rows2 + c * own
                packed = stats[at_row : at_row + 8]
                for g in range(1, groups):
                    piece = stats[at_row + 8 * g : at_row + 8 * g + 8]
                    piece = pltpu.roll(piece, 2 * heads * g, 1)
                    packed = jnp.where(lane[0:8] >= 2 * heads * g, piece, packed)
                st_send[2 * duo + c] = packed
        for d in duos:
            for x in (2 * d + 1, 2 * d):
                if x:
                    target = flip(me_b, x)
                    ba_copy(st_send.at[target], st_recv.at[x - 1], st_sems, x).start()
                    ba_copy(o_send.at[target], o_recv.at[x - 1], o_sems, x).start()

    lane = lax.broadcasted_iota(jnp.int32, (own, LANES), 1)

    def unpack(packed):
        parts = [packed]
        for g in range(1, groups):
            parts.append(pltpu.roll(packed, LANES - 2 * heads * g, 1))
        return jnp.concatenate(parts, axis=0)

    take(st_recv, st_sems.at[1])
    tops = []
    for d in range(chips):
        mine = st_recv[2 * d - 1] if d else st_send[me_b]
        tops.append(unpack(mine + st_recv[2 * d]))
    overall = tops[0]
    for top in tops[1:]:
        overall = jnp.maximum(overall, top)
    factors = [jnp.exp(top - overall) for top in tops]
    denominator = jnp.zeros((own, LANES), F32)
    for factor, top in zip(factors, tops):
        denominator = denominator + factor * pltpu.roll(top, LANES - heads, 1)
    head_row = lax.broadcasted_iota(jnp.int32, (LANES, width), 0)
    head_lane = lax.broadcasted_iota(jnp.int32, (LANES, width), 1)
    inside = (head_lane >= head_row * head_dim) & (head_lane < (head_row + 1) * head_dim)
    spread = jnp.where(inside, 1.0, 0.0).astype(BF16)
    live = lane < heads
    shares = jnp.concatenate(
        [jnp.where(live, factor / denominator, 0.0) for factor in factors], axis=0
    )
    coarse = shares.astype(BF16)
    fine = (shares - coarse.astype(F32)).astype(BF16)
    wide = dot(coarse, spread) + dot(fine, spread)
    take(o_recv, o_sems.at[1])
    left = jnp.zeros((own, span), F32)
    right = jnp.zeros((own, span), F32)
    for d in range(chips):
        mine = (o_recv[2 * d - 1] if d else o_send[me_b]).astype(F32)
        other = o_recv[2 * d].astype(F32)
        part = wide[d * own : (d + 1) * own]
        left = left + part[:, 0:span] * jnp.where(core == 0, mine, other)
        right = right + part[:, span:width] * jnp.where(core == 0, other, mine)
    attended = jnp.concatenate([left, right], axis=1)
    mixed = (attended * gate.astype(F32)).astype(BF16)
    loaded("wod", v_wod)
    tokens_mid = v_tok[...] + dot(mixed, v_wod[0:width, :])
    normed_mid = norm(tokens_mid, gains_ref[1:2, :]).astype(BF16)
    loaded("wup", v_wup)
    part = 512
    for n in range(0, hidden, part):
        first = dot(normed_mid, v_wup[:, n : n + part])
        second = dot(normed_mid, v_wup[:, hidden + n : hidden + n + part])
        v_inner[:, n : n + part] = (first * jax.nn.sigmoid(first) * second).astype(BF16)
    outs = []

    def share(c):
        columns_c = pl.ds(c * span, span)
        for d in chip_order:
            ba_copy(
                t_own.at[:, columns_c], t_all.at[me_b, :, columns_c], t_sems, 2 * d, d
            ).start()

    for c in range(2):
        out = dot(v_inner[...], v_wod[width : width + hidden, c * span : (c + 1) * span])
        out = tokens_mid[:, c * span : (c + 1) * span] + out
        outs.append(out)
        t_own[:, c * span : (c + 1) * span] = out.astype(BF16)
        t_all[me_b, :, c * span : (c + 1) * span] = out.astype(BF16)
        if c == 0:
            share(0)
    token_out = jnp.concatenate(outs, axis=1)
    loaded("wta", v_wta)
    normed_out = norm(token_out, gains_ref[2:3, :]).astype(BF16)
    token_atom = dot(normed_out, v_wta[...]).astype(BF16)
    ta_own[...] = token_atom
    ta_all[me_b] = token_atom
    for x in order:
        ba_copy(ta_own, ta_all.at[me_b], ta_sems, x).start()
    share(1)
    ba_copy(t_own, t_all.at[me_b], tm_sems, 1).start()
    loaded("w_pos_out", w_pos_out_ref)
    ta_pieces = ta_all.at[pl.ds(0, n_ba - 1)]
    take(ta_pieces, ta_sems.at[1])
    for d in range(1, chips):
        rows = t_all.at[flip(me_b, 2 * d)]
        take(rows, t_sems.at[d])
        ba_copy(rows, rows, tm_sems, 1).start()
    picked = dot(v_onehot[...], ta_all[...].reshape(tok_rows, channels))
    atom_normed = norm(v_state[...] + picked, None).astype(BF16)
    update = dot_nt(w_pos_out_ref[...], atom_normed)[:, 0:atoms]
    den_ref[...] = noisy_ref[...] * (inv_scale * inv_scale) + update * (sigma * inv_scale)
    t_pieces = t_all.at[pl.ds(0, chips)]
    take(t_pieces, tm_sems.at[1])
    for whole, sem in (
        (state_mate, state_sems),
        (ids_mate, ids_mate_sems),
        (ids_all, ids_sems),
        (sum_recv, sum_sems),
        (bias_send, bias_sems),
        (chip_pieces, kvm_sems),
        (q_pieces, q_sems),
        (st_recv, st_sems),
        (o_recv, o_sems),
        (t_all.at[pl.ds(0, chips - 1)], t_sems),
        (t_pieces, tm_sems),
        (ta_pieces, ta_sems),
    ):
        take(whole, sem.at[0])
    take(rows_kv.at[pl.ds(0, n_aa - 1)], kv_send.at[1])

    @pl.when(column != me_b)
    def _():
        take(rows_own, kv_send.at[0])


def finish_kernel(tok_ref, den_ref, den_out_ref, tok_out_ref):
    den_out_ref[...] = den_ref[...]
    tok_out_ref[...] = tok_ref[...].astype(F32)


def on_device(
    n_aa,
    n_ba,
    atom_cond,
    noisy_pos,
    noise_level,
    atom_token,
    token_cond,
    pair,
    pair_bias_weight,
    gains,
    w_pos,
    w_atom_token,
    w_query_gate,
    w_key_value,
    w_attn_out,
    w_up,
    w_down,
    w_token_atom,
    w_pos_out,
):
    atoms, channels = atom_cond.shape
    atoms_pad = -(-atoms // LANES) * LANES
    tok_rows, width = token_cond.shape
    cols = pair.shape[1]
    heads = pair_bias_weight.shape[0]
    own = tok_rows // n_ba
    chips = n_ba // 2
    half, span, keys_n = heads // 2, width // 2, 2 * cols
    part_rows = 8
    parts = own // part_rows
    head_dim = width // heads
    if tok_rows != 2 * cols or chips != n_aa:
        raise ValueError("unsupported mesh")
    tile_heads = max(
        (t * LANES + LANES - 1) // head_dim - t * LANES // head_dim + 1
        for t in range(span // LANES)
    )
    ids = atom_token
    if atoms_pad > atoms:
        ids = jnp.pad(atom_token, (0, atoms_pad - atoms), constant_values=-1)
    vmem = pl.BlockSpec(memory_space=pltpu.VMEM)
    smem = pl.BlockSpec(memory_space=pltpu.SMEM)
    hbm = pl.BlockSpec(memory_space=pltpu.HBM)
    dma = pltpu.SemaphoreType.DMA
    operands = [
        pltpu.with_memory_space_constraint(value, pltpu.HBM) if value.size > 1 else value
        for value in (
            atom_cond,
            noisy_pos,
            noise_level,
            ids,
            token_cond,
            pair,
            pair_bias_weight,
            gains,
            w_pos,
            w_atom_token,
            w_query_gate,
            w_key_value,
            w_attn_out,
            w_up,
            w_down,
            w_token_atom,
            w_pos_out,
        )
    ]
    denoised, tokens = pl.pallas_call(
        functools.partial(step_kernel, n_aa, n_ba),
        out_shape=[
            jax.ShapeDtypeStruct((3, atoms), F32),
            jax.ShapeDtypeStruct((n_ba, own, width), BF16),
        ],
        in_specs=[hbm, hbm, smem] + [hbm] * 14,
        out_specs=[vmem, vmem],
        scratch_shapes=[
            pltpu.VMEM((3, atoms), F32),
            pltpu.VMEM(pair_bias_weight.shape, BF16),
            pltpu.VMEM(gains.shape, F32),
            pltpu.VMEM(w_pos.shape, F32),
            pltpu.VMEM(w_pos_out.shape, BF16),
            pltpu.VMEM((atoms_pad, channels), F32),
            pltpu.VMEM((LANES, atoms_pad), F32),
            pltpu.VMEM((atoms_pad, tok_rows), BF16),
            pltpu.VMEM((own, width), F32),
            pltpu.VMEM(pair.shape, BF16),
            pltpu.VMEM((2, tok_rows * half, cols), F32),
            pltpu.VMEM((tok_rows * half, cols), F32),
            pltpu.VMEM(w_atom_token.shape, BF16),
            pltpu.VMEM(w_query_gate.shape, BF16),
            pltpu.VMEM((width, width), BF16),
            pltpu.VMEM((width + w_down.shape[0], width), BF16),
            pltpu.VMEM(w_up.shape, BF16),
            pltpu.VMEM(w_token_atom.shape, BF16),
            pltpu.VMEM((1, atoms_pad), jnp.int32),
            pltpu.VMEM((1, atoms_pad), jnp.int32),
            pltpu.VMEM((n_ba - 1, 1, atoms_pad), jnp.int32),
            pltpu.VMEM((atoms_pad, channels), BF16),
            pltpu.VMEM((atoms_pad, channels), BF16),
            pltpu.VMEM((parts, chips, part_rows, width), BF16),
            pltpu.VMEM((parts, chips - 1, part_rows, width), BF16),
            pltpu.VMEM((parts, part_rows, width), BF16),
            pltpu.VMEM((n_ba, parts, part_rows, width), BF16),
            pltpu.VMEM((2, own, span), BF16),
            pltpu.VMEM((n_ba, own, span), BF16),
            pltpu.VMEM((half, keys_n, 2 * LANES), BF16),
            pltpu.VMEM((span // LANES, tile_heads, keys_n, LANES), BF16),
            pltpu.VMEM((4 * own, half * keys_n), BF16),
            pltpu.VMEM((n_ba, own, span), BF16),
            pltpu.VMEM((n_ba - 1, own, span), BF16),
            pltpu.VMEM((n_ba, 8, LANES), F32),
            pltpu.VMEM((n_ba - 1, 8, LANES), F32),
            pltpu.VMEM((own, w_down.shape[0]), BF16),
            pltpu.VMEM((own, width), BF16),
            pltpu.VMEM((own, channels), BF16),
            pltpu.VMEM((n_ba, own, channels), BF16),
            dma((14,)),
            dma((PAIR_CHUNKS,)),
            dma((2,)),
            dma((2,)),
            dma((2,)),
            dma((1 + parts,)),
            dma((2,)),
            dma((2,)),
            dma((parts, chips)),
            dma((2,)),
            dma((2,)),
            dma((2,)),
            dma((2,)),
            dma((chips,)),
            dma((2,)),
            dma((2,)),
        ],
        compiler_params=pltpu.CompilerParams(
            collective_id=0, has_side_effects=True, vmem_limit_bytes=48 * 1024 * 1024
        ),
    )(*operands)
    denoised, token_out = pl.pallas_call(
        finish_kernel,
        out_shape=[
            jax.ShapeDtypeStruct((3, atoms), F32),
            jax.ShapeDtypeStruct((tok_rows, width), F32),
        ],
        in_specs=[vmem, vmem],
        out_specs=[vmem, vmem],
        compiler_params=pltpu.CompilerParams(vmem_limit_bytes=8 * 1024 * 1024),
    )(tokens.reshape(tok_rows, width), denoised)
    return denoised, token_out


def solution(mesh):
    in_specs = (
        P(("aa", "ba"), None),
        P(None, ("aa", "ba")),
        P(),
        P(("aa", "ba")),
        P("aa", None),
        P("aa", "ba", None),
    ) + (P(),) * 11
    out_specs = (P(None, ("aa", "ba")), P("aa", None))
    return jax.shard_map(
        functools.partial(on_device, mesh.shape["aa"], mesh.shape["ba"]),
        mesh=mesh,
        in_specs=in_specs,
        out_specs=out_specs,
        check_vma=False,
    )
```

```python
import functools

import jax
import jax.numpy as jnp
from jax import lax
from jax.experimental import pallas as pl
from jax.experimental.pallas import tpu as pltpu
from jax.sharding import PartitionSpec as P

MESH = pl.DeviceIdType.MESH
F32 = jnp.float32
BF16 = jnp.bfloat16
LANES = 128
PAIR_CHUNKS = 8
EARLY_CHUNKS = 3
BIAS_ROWS = 8


def flip(index, mask):
    out = index
    bit = 1
    while bit <= mask:
        if mask & bit:
            out = out + bit - 2 * bit * lax.rem(index // bit, 2)
        bit *= 2
    return out


def far_first(count):
    return sorted(range(1, count), key=lambda m: (-bin(m).count("1"), m))


def norm(values, gain_row):
    mean_value = jnp.mean(values, axis=-1, keepdims=True)
    centered = values - mean_value
    variance = jnp.mean(centered * centered, axis=-1, keepdims=True)
    scaled = centered * lax.rsqrt(variance + 1e-05)
    return scaled if gain_row is None else scaled * gain_row


def dot(a, b):
    return jnp.dot(a, b, preferred_element_type=F32)


def dot_nt(a, b):
    return lax.dot_general(a, b, (((1,), (1,)), ((), ())), preferred_element_type=F32)


def step_kernel(
    n_aa,
    n_ba,
    atom_hbm,
    noisy_hbm,
    noise_ref,
    ids_hbm,
    tok_hbm,
    pair_hbm,
    bias_w_hbm,
    gains_hbm,
    w_pos_hbm,
    wat_hbm,
    wqg_hbm,
    wkv_hbm,
    wo_hbm,
    wup_hbm,
    wdn_hbm,
    wta_hbm,
    w_pos_out_hbm,
    den_ref,
    t_all,
    noisy_ref,
    bias_w_ref,
    gains_ref,
    w_pos_ref,
    w_pos_out_ref,
    v_state,
    v_post,
    v_onehot,
    v_tok,
    v_pair,
    v_bias,
    bias_send,
    v_wat,
    v_wqg,
    v_wkv,
    v_wod,
    v_wup,
    v_wta,
    v_ids,
    ids_mate,
    ids_all,
    state_own,
    state_mate,
    sum_send,
    sum_recv,
    rows_own,
    rows_kv,
    q_own,
    q_all,
    v_km,
    v_vm,
    v_p,
    o_send,
    o_recv,
    st_send,
    st_recv,
    v_inner,
    t_own,
    ta_own,
    ta_all,
    load_sem,
    pair_sem,
    ids_mate_sems,
    ids_sems,
    state_sems,
    sum_sems,
    bias_sems,
    kv_send,
    kv_recv,
    kvm_sems,
    q_sems,
    o_sems,
    st_sems,
    t_sems,
    tm_sems,
    ta_sems,
):
    atoms = noisy_ref.shape[1]
    atoms_pad = v_state.shape[0]
    tok_rows, cols, channels = v_pair.shape
    heads = bias_w_ref.shape[0]
    half = heads // 2
    own, width = v_tok.shape
    head_dim = width // heads
    span = width // 2
    hidden = v_wod.shape[0] - width
    parts, part_rows = rows_own.shape[:2]
    chips = n_ba // 2
    keys_n = 2 * cols
    me_a = lax.axis_index("aa")
    me_b = lax.axis_index("ba")
    core = lax.rem(me_b, 2)
    chip = me_b // 2

    own_start = pl.multiple_of(me_b * own, own)
    span_start = pl.multiple_of(core * span, LANES)
    copies = [
        ("ids", ids_hbm, v_ids.at[0]),
        ("noisy", noisy_hbm, noisy_ref),
        ("atom", atom_hbm, v_state.at[pl.ds(0, atoms)]),
        ("w_pos", w_pos_hbm, w_pos_ref),
        ("wat", wat_hbm, v_wat),
        ("bias_w", bias_w_hbm, bias_w_ref),
        ("gains", gains_hbm, gains_ref),
        ("tok", tok_hbm.at[pl.ds(own_start, own)], v_tok),
        ("w_pos_out", w_pos_out_hbm, w_pos_out_ref),
        ("wqg", wqg_hbm, v_wqg),
        ("wkv", wkv_hbm.at[:, pl.ds(span_start, span)], v_wkv.at[:, pl.ds(0, span)]),
        (
            "wkv",
            wkv_hbm.at[:, pl.ds(pl.multiple_of(width + core * span, LANES), span)],
            v_wkv.at[:, pl.ds(span, span)],
        ),
        ("wod", wo_hbm, v_wod.at[pl.ds(0, width)]),
        ("wup", wup_hbm, v_wup),
        ("wod", wdn_hbm, v_wod.at[pl.ds(width, hidden)]),
        ("wta", wta_hbm, v_wta),
    ]
    names = list(dict.fromkeys(name for name, _, _ in copies))

    def load(name):
        for key, src, dst in copies:
            if key == name:
                pltpu.make_async_copy(src, dst, load_sem.at[names.index(name)]).start()

    def take(whole, sem):
        pltpu.make_async_copy(whole, whole, sem).wait()

    def loaded(name, whole):
        take(whole, load_sem.at[names.index(name)])

    step = tok_rows // PAIR_CHUNKS
    pair_loads = [
        pltpu.make_async_copy(
            pair_hbm.at[pl.ds(c * step, 2 * step)],
            v_pair.at[pl.ds(c * step, 2 * step)],
            pair_sem.at[c // 2],
        )
        for c in range(0, PAIR_CHUNKS, 2)
    ]
    for name in names[:5]:
        load(name)

    def at(a, b):
        return {"aa": a, "ba": b}

    def greet(device):
        pl.semaphore_signal(barrier, inc=1, device_id=device, device_id_type=MESH)

    barrier = pltpu.get_barrier_semaphore()
    for x in range(1, n_ba):
        greet(at(me_a, flip(me_b, x)))
    block = me_b // chips
    column = 2 * me_a + block
    for x in range(1, n_aa):
        greet(at(flip(me_a, x), column))

    @pl.when(chip != me_a)
    def _():
        for j in range(chips):
            greet(at(chip, core * chips + j))

    greetings = n_ba - 1 + n_aa - 1 + jnp.where(chip != me_a, chips, 0)

    for name in names[5:8]:
        load(name)
    for copy in pair_loads:
        copy.start()
    for name in names[8:]:
        load(name)
    if atoms_pad > atoms:
        v_state[pl.ds(atoms, atoms_pad - atoms), :] = jnp.zeros(
            (atoms_pad - atoms, channels), F32
        )

    def ba_copy(src, dst, sems, x, slot=1):
        return pltpu.make_async_remote_copy(
            src_ref=src,
            dst_ref=dst,
            send_sem=sems.at[0],
            recv_sem=sems.at[slot],
            device_id=at(me_a, flip(me_b, x)),
            device_id_type=MESH,
        )

    order = far_first(n_ba)
    chip_order = far_first(chips)

    loaded("noisy", noisy_ref)
    sigma = jnp.full((3, atoms), noise_ref[0], F32)
    inv_scale = 1.0 / jnp.sqrt(sigma * sigma + 1.0)
    v_post[...] = jnp.full(v_post.shape, -1.0, F32)
    v_post[0:3, 0:atoms] = noisy_ref[...] * inv_scale
    loaded("ids", v_ids.at[0])
    ids_row = v_ids[...]
    v_post[3:4, :] = ids_row.astype(F32)
    columns = v_post[...].T
    loaded("w_pos", w_pos_ref)
    loaded("atom", v_state.at[pl.ds(0, atoms)])
    state = v_state[...]
    for c in range(3):
        state = state + columns[:, c : c + 1] * w_pos_ref[c : c + 1, :]
    v_state[...] = state
    rounded = state.astype(BF16)
    state_own[...] = rounded

    pl.semaphore_wait(barrier, greetings)
    ba_copy(state_own, state_mate, state_sems, 1).start()
    ba_copy(v_ids, ids_mate, ids_mate_sems, 1).start()
    for x in order:
        ba_copy(v_ids, ids_all.at[x - 1], ids_sems, x).start()
    group = max(1, parts // 2)

    def select(ids, first):
        row = lax.broadcasted_iota(jnp.int32, (group * chips * part_rows, atoms_pad), 0)
        token = lax.rem(row, part_rows) + 2 * own * lax.rem(row // part_rows, chips)
        token = token + part_rows * (first + row // (part_rows * chips))
        token = token + (own * core + me_a * tok_rows)
        return jnp.where(token == ids, 1.0, 0.0).astype(BF16)

    loaded("wat", v_wat)
    hidden_own = jnp.maximum(dot(rounded, v_wat[...]), 0.0).astype(BF16)
    firsts = range(0, parts, group)
    own_sums = [dot(select(ids_row, first), hidden_own) for first in firsts]
    take(ids_mate, ids_mate_sems.at[1])
    selectors = [select(ids_mate[...], first) for first in firsts]
    take(state_mate, state_sems.at[1])
    hidden_mate = jnp.maximum(dot(state_mate[...], v_wat[...]), 0.0).astype(BF16)
    for first, sums, selector in zip(firsts, own_sums, selectors):
        chip_sums = sums + dot(selector, hidden_mate)
        sum_send[first : first + group] = chip_sums.astype(BF16).reshape(
            group, chips, part_rows, width
        )
        for part in range(first, first + group):
            for d in chip_order:
                ba_copy(
                    sum_send.at[part, flip(chip, d)],
                    sum_recv.at[part, d - 1],
                    sum_sems,
                    2 * d,
                    1 + part,
                ).start()

    lane_id = lax.broadcasted_iota(jnp.int32, (atoms_pad, tok_rows), 1) + me_a * tok_rows
    v_onehot[...] = jnp.where(columns[:, 3:4] == lane_id.astype(F32), 1.0, 0.0).astype(BF16)
    loaded("bias_w", bias_w_ref)
    weights_all = bias_w_ref[...].astype(F32)
    first_half, second_half = weights_all[0:half], weights_all[half:heads]
    bias_w = jnp.concatenate(
        [
            jnp.where(core == 0, first_half, second_half),
            jnp.where(core == 0, second_half, first_half),
        ],
        axis=0,
    ).astype(BF16)
    bias_rows = step * half
    bias_copies = [
        ba_copy(
            bias_send.at[pl.ds(c * bias_rows, bias_rows)],
            v_bias.at[core, pl.ds(c * bias_rows, bias_rows)],
            bias_sems,
            1,
        )
        for c in range(PAIR_CHUNKS)
    ]

    def bias_chunk(c):
        if c % 2 == 0:
            pair_loads[c // 2].wait()

        def rows(r, carry):
            start = c * step + r * BIAS_ROWS
            block = v_pair[pl.ds(start, BIAS_ROWS)].reshape(BIAS_ROWS * cols, channels)
            out = dot_nt(bias_w, block)
            for i in range(BIAS_ROWS):
                where = pl.ds(pl.multiple_of((start + i) * half, half), half)
                v_bias[core, where, :] = out[0:half, i * cols : (i + 1) * cols]
                bias_send[where, :] = out[half:heads, i * cols : (i + 1) * cols]
            return carry

        lax.fori_loop(0, step // BIAS_ROWS, rows, 0)
        bias_copies[c].start()

    for c in range(EARLY_CHUNKS):
        bias_chunk(c)

    own_row = lax.broadcasted_iota(jnp.int32, (own, atoms_pad), 0) + (
        me_a * tok_rows + me_b * own
    )
    take(ids_all, ids_sems.at[1])
    hits = jnp.where(own_row == ids_row, 1.0, 0.0)
    for x in order:
        hits = hits + jnp.where(own_row == ids_all[x - 1], 1.0, 0.0)
    counts = jnp.sum(hits, axis=1, keepdims=True)
    loaded("tok", v_tok)
    loaded("gains", gains_ref)

    low = jnp.where(2 * me_a < n_aa, me_a, n_aa - 1 - me_a)

    def plane(k):
        if k < 0:
            return me_a
        place = n_aa - 1 - k
        place = jnp.where(place > low, place, k - (n_aa - 1 - low))
        return jnp.where(2 * me_a < n_aa, place, n_aa - 1 - place)

    def kv_copy(k, part):
        return pltpu.make_async_remote_copy(
            src_ref=rows_own.at[part],
            dst_ref=rows_kv.at[me_b, part],
            send_sem=kv_send.at[1 if k >= 0 else 0],
            recv_sem=kv_recv.at[part],
            device_id=at(plane(k), column),
            device_id_type=MESH,
        )

    for part in range(parts):
        rows = pl.ds(part * part_rows, part_rows)
        summed = sum_send[part, chip].astype(F32)
        take(sum_recv.at[part], sum_sems.at[1 + part])
        for d in chip_order:
            summed = summed + sum_recv[part, d - 1].astype(F32)
        tokens_start = (
            v_tok[rows, :] + summed / counts[part * part_rows : (part + 1) * part_rows]
        )
        v_tok[rows, :] = tokens_start
        rows_own[part] = norm(tokens_start, gains_ref[0:1, :]).astype(BF16)
        for k in range(n_aa - 1):
            kv_copy(k, part).start()

        @pl.when(column != me_b)
        def _():
            kv_copy(-1, part).start()

        @pl.when(column == me_b)
        def _():
            pltpu.make_async_copy(
                rows_own.at[part], rows_kv.at[me_b, part], kv_recv.at[part]
            ).start()

    normed = rows_own[...].reshape(own, width)
    loaded("wqg", v_wqg)
    query = dot(normed, v_wqg[:, 0:width]).astype(BF16)
    for c in range(2):
        q_own[c] = query[:, c * span : (c + 1) * span]
    q_all[me_b] = q_own[core]
    gate = jax.nn.sigmoid(dot(normed, v_wqg[:, width : 2 * width])).astype(BF16)

    for c in range(EARLY_CHUNKS, PAIR_CHUNKS):
        bias_chunk(c)
        if c == EARLY_CHUNKS + 1:
            for x in order:
                ba_copy(q_own.at[lax.rem(core + x, 2)], q_all.at[me_b], q_sems, x).start()
    for part in range(parts):
        rows = rows_kv.at[pl.ds(core * chips, chips), part]
        take(rows, kv_recv.at[part])
        ba_copy(rows, rows, kvm_sems, 1).start()
    loaded("wkv", v_wkv)
    chip_pieces = rows_kv.at[pl.ds(0, chips)]
    spans = []
    for h in range(half):
        lo = h * head_dim // LANES * LANES
        hi = ((h + 1) * head_dim + LANES - 1) // LANES * LANES
        spans.append((lo, hi))
    tiles = []
    for t in range(span // LANES):
        tiles.append((t * LANES // head_dim, (t * LANES + LANES - 1) // head_dim))

    def project(which):
        pieces = rows_kv[pl.ds(which * chips, chips)].reshape(cols, width)
        key_value = dot(pieces, v_wkv[...])
        keys = pl.ds(pl.multiple_of(which * cols, cols), cols)
        turned = [
            key_value[:, t * LANES : (t + 1) * LANES].T for t in range(span // LANES)
        ]
        for h, (lo, hi) in enumerate(spans):
            for t in range(lo // LANES, hi // LANES):
                row = lax.broadcasted_iota(jnp.int32, (LANES, cols), 0) + t * LANES
                mine = (row >= h * head_dim) & (row < (h + 1) * head_dim)
                v_km[h, t * LANES - lo : (t + 1) * LANES - lo, keys] = jnp.where(
                    mine, turned[t], 0.0
                ).astype(BF16)
        for t, (h0, h1) in enumerate(tiles):
            piece = key_value[:, span + t * LANES : span + (t + 1) * LANES]
            lane = lax.broadcasted_iota(jnp.int32, (cols, LANES), 1) + t * LANES
            for h in range(h0, h1 + 1):
                mine = (lane >= h * head_dim) & (lane < (h + 1) * head_dim)
                v_vm[t, h - h0, keys, :] = jnp.where(mine, piece, 0.0).astype(BF16)

    project(core)
    take(chip_pieces, kvm_sems.at[1])
    project(1 - core)

    q_pieces = q_all.at[pl.ds(0, n_ba - 1)]
    take(q_pieces, q_sems.at[1])
    take(bias_send, bias_sems.at[1])

    scale = head_dim ** (-0.5)
    rows2 = 2 * own
    batches = [chip_order[:1]] + [chip_order[n : n + 2] for n in range(1, chips - 1, 2)] + [[0]]
    groups = own // 8
    for duos in batches:
        places = [flip(chip, d) for d in duos]
        many = len(places)
        lane = lax.broadcasted_iota(jnp.int32, (many * rows2, LANES), 1)
        top_lane = lane - half * core
        stats = jnp.zeros((many * rows2, LANES), F32)
        q_rows = jnp.concatenate(
            [q_all[pl.ds(2 * duo, 2)].reshape(rows2, span) for duo in places], axis=0
        )
        for h in range(half):
            lo, hi = spans[h]
            scores = dot(q_rows[:, lo:hi], v_km[h, 0 : hi - lo, :]) * scale
            pair_bias = [
                jnp.concatenate(
                    [
                        v_bias[k, pl.ds(duo * (rows2 * half) + h, rows2, stride=half), :]
                        for duo in places
                    ],
                    axis=0,
                )
                for k in range(2)
            ]
            both = [scores[:, k * cols : (k + 1) * cols] + pair_bias[k] for k in range(2)]
            top = jnp.max(jnp.maximum(both[0], both[1]), axis=1, keepdims=True)
            both = [jnp.exp(one - top) for one in both]
            total = jnp.sum(both[0] + both[1], axis=1, keepdims=True)
            stats = jnp.where(top_lane == h, top, stats)
            stats = jnp.where(top_lane == heads + h, total, stats)
            for k in range(2):
                v_p[0 : many * rows2, h * keys_n + k * cols : h * keys_n + (k + 1) * cols] = both[k].astype(BF16)
        for t, (h0, h1) in enumerate(tiles):
            count = (h1 - h0 + 1) * keys_n
            out = dot(
                v_p[0 : many * rows2, h0 * keys_n : h0 * keys_n + count],
                v_vm[t, 0 : h1 - h0 + 1].reshape(count, LANES),
            ).astype(BF16)
            for i, duo in enumerate(places):
                o_send[pl.ds(2 * duo, 2), :, t * LANES : (t + 1) * LANES] = out[
                    i * rows2 : (i + 1) * rows2
                ].reshape(2, own, LANES)
        for i, duo in enumerate(places):
            for c in range(2):
                at_row = i * rows2 + c * own
                packed = stats[at_row : at_row + 8]
                for g in range(1, groups):
                    piece = stats[at_row + 8 * g : at_row + 8 * g + 8]
                    piece = pltpu.roll(piece, 2 * heads * g, 1)
                    packed = jnp.where(lane[0:8] >= 2 * heads * g, piece, packed)
                st_send[2 * duo + c] = packed
        for d in duos:
            for x in (2 * d + 1, 2 * d):
                if x:
                    target = flip(me_b, x)
                    ba_copy(st_send.at[target], st_recv.at[x - 1], st_sems, x).start()
                    ba_copy(o_send.at[target], o_recv.at[x - 1], o_sems, x).start()

    lane = lax.broadcasted_iota(jnp.int32, (own, LANES), 1)

    def unpack(packed):
        parts = [packed]
        for g in range(1, groups):
            parts.append(pltpu.roll(packed, LANES - 2 * heads * g, 1))
        return jnp.concatenate(parts, axis=0)

    take(st_recv, st_sems.at[1])
    tops = []
    for d in range(chips):
        mine = st_recv[2 * d - 1] if d else st_send[me_b]
        tops.append(unpack(mine + st_recv[2 * d]))
    overall = tops[0]
    for top in tops[1:]:
        overall = jnp.maximum(overall, top)
    factors = [jnp.exp(top - overall) for top in tops]
    denominator = jnp.zeros((own, LANES), F32)
    for factor, top in zip(factors, tops):
        denominator = denominator + factor * pltpu.roll(top, LANES - heads, 1)
    head_row = lax.broadcasted_iota(jnp.int32, (LANES, width), 0)
    head_lane = lax.broadcasted_iota(jnp.int32, (LANES, width), 1)
    inside = (head_lane >= head_row * head_dim) & (head_lane < (head_row + 1) * head_dim)
    spread = jnp.where(inside, 1.0, 0.0).astype(BF16)
    live = lane < heads
    shares = jnp.concatenate(
        [jnp.where(live, factor / denominator, 0.0) for factor in factors], axis=0
    )
    coarse = shares.astype(BF16)
    fine = (shares - coarse.astype(F32)).astype(BF16)
    wide = dot(coarse, spread) + dot(fine, spread)
    take(o_recv, o_sems.at[1])
    left = jnp.zeros((own, span), F32)
    right = jnp.zeros((own, span), F32)
    for d in range(chips):
        mine = (o_recv[2 * d - 1] if d else o_send[me_b]).astype(F32)
        other = o_recv[2 * d].astype(F32)
        part = wide[d * own : (d + 1) * own]
        left = left + part[:, 0:span] * jnp.where(core == 0, mine, other)
        right = right + part[:, span:width] * jnp.where(core == 0, other, mine)
    attended = jnp.concatenate([left, right], axis=1)
    mixed = (attended * gate.astype(F32)).astype(BF16)
    loaded("wod", v_wod)
    tokens_mid = v_tok[...] + dot(mixed, v_wod[0:width, :])
    normed_mid = norm(tokens_mid, gains_ref[1:2, :]).astype(BF16)
    loaded("wup", v_wup)
    part = 512
    for n in range(0, hidden, part):
        first = dot(normed_mid, v_wup[:, n : n + part])
        second = dot(normed_mid, v_wup[:, hidden + n : hidden + n + part])
        v_inner[:, n : n + part] = (first * jax.nn.sigmoid(first) * second).astype(BF16)
    outs = []

    def share(c):
        columns_c = pl.ds(c * span, span)
        for d in chip_order:
            ba_copy(
                t_own.at[:, columns_c],
                t_all.at[me_b, :, columns_c],
                t_sems,
                2 * d,
                c * (chips - 1) + d,
            ).start()

    for c in range(2):
        out = dot(v_inner[...], v_wod[width : width + hidden, c * span : (c + 1) * span])
        out = tokens_mid[:, c * span : (c + 1) * span] + out
        outs.append(out)
        t_own[:, c * span : (c + 1) * span] = out.astype(BF16)
        t_all[me_b, :, c * span : (c + 1) * span] = out.astype(BF16)
        if c == 0:
            share(0)
    token_out = jnp.concatenate(outs, axis=1)
    loaded("wta", v_wta)
    normed_out = norm(token_out, gains_ref[2:3, :]).astype(BF16)
    token_atom = dot(normed_out, v_wta[...]).astype(BF16)
    ta_own[...] = token_atom
    ta_all[me_b] = token_atom
    for x in order:
        ba_copy(ta_own, ta_all.at[me_b], ta_sems, x).start()
    share(1)
    ba_copy(t_own, t_all.at[me_b], tm_sems, 1).start()
    loaded("w_pos_out", w_pos_out_ref)
    for c in range(2):
        for d in range(1, chips):
            rows = t_all.at[flip(me_b, 2 * d), :, pl.ds(c * span, span)]
            take(rows, t_sems.at[c * (chips - 1) + d])
            ba_copy(rows, rows, tm_sems, 1).start()
    ta_pieces = ta_all.at[pl.ds(0, n_ba - 1)]
    take(ta_pieces, ta_sems.at[1])
    picked = dot(v_onehot[...], ta_all[...].reshape(tok_rows, channels))
    atom_normed = norm(v_state[...] + picked, None).astype(BF16)
    update = dot_nt(w_pos_out_ref[...], atom_normed)[:, 0:atoms]
    den_ref[...] = noisy_ref[...] * (inv_scale * inv_scale) + update * (sigma * inv_scale)
    t_pieces = t_all.at[pl.ds(0, chips)]
    take(t_pieces, tm_sems.at[1])
    for whole, sem in (
        (state_mate, state_sems),
        (ids_mate, ids_mate_sems),
        (ids_all, ids_sems),
        (sum_recv, sum_sems),
        (bias_send, bias_sems),
        (chip_pieces, kvm_sems),
        (q_pieces, q_sems),
        (st_recv, st_sems),
        (o_recv, o_sems),
        (t_all.at[pl.ds(0, chips - 1)], t_sems),
        (t_pieces, tm_sems),
        (ta_pieces, ta_sems),
    ):
        take(whole, sem.at[0])
    take(rows_kv.at[pl.ds(0, n_aa - 1)], kv_send.at[1])

    @pl.when(column != me_b)
    def _():
        take(rows_own, kv_send.at[0])


def finish_kernel(tok_ref, den_ref, den_out_ref, tok_out_ref):
    den_out_ref[...] = den_ref[...]
    tok_out_ref[...] = tok_ref[...].astype(F32)


def on_device(
    n_aa,
    n_ba,
    atom_cond,
    noisy_pos,
    noise_level,
    atom_token,
    token_cond,
    pair,
    pair_bias_weight,
    gains,
    w_pos,
    w_atom_token,
    w_query_gate,
    w_key_value,
    w_attn_out,
    w_up,
    w_down,
    w_token_atom,
    w_pos_out,
):
    atoms, channels = atom_cond.shape
    atoms_pad = -(-atoms // LANES) * LANES
    tok_rows, width = token_cond.shape
    cols = pair.shape[1]
    heads = pair_bias_weight.shape[0]
    own = tok_rows // n_ba
    chips = n_ba // 2
    half, span, keys_n = heads // 2, width // 2, 2 * cols
    part_rows = min(16, own)
    parts = own // part_rows
    head_dim = width // heads
    if tok_rows != 2 * cols or chips != n_aa:
        raise ValueError("unsupported mesh")
    tile_heads = max(
        (t * LANES + LANES - 1) // head_dim - t * LANES // head_dim + 1
        for t in range(span // LANES)
    )
    ids = atom_token
    if atoms_pad > atoms:
        ids = jnp.pad(atom_token, (0, atoms_pad - atoms), constant_values=-1)
    vmem = pl.BlockSpec(memory_space=pltpu.VMEM)
    smem = pl.BlockSpec(memory_space=pltpu.SMEM)
    hbm = pl.BlockSpec(memory_space=pltpu.HBM)
    dma = pltpu.SemaphoreType.DMA
    operands = [
        pltpu.with_memory_space_constraint(value, pltpu.HBM) if value.size > 1 else value
        for value in (
            atom_cond,
            noisy_pos,
            noise_level,
            ids,
            token_cond,
            pair,
            pair_bias_weight,
            gains,
            w_pos,
            w_atom_token,
            w_query_gate,
            w_key_value,
            w_attn_out,
            w_up,
            w_down,
            w_token_atom,
            w_pos_out,
        )
    ]
    denoised, tokens = pl.pallas_call(
        functools.partial(step_kernel, n_aa, n_ba),
        out_shape=[
            jax.ShapeDtypeStruct((3, atoms), F32),
            jax.ShapeDtypeStruct((n_ba, own, width), BF16),
        ],
        in_specs=[hbm, hbm, smem] + [hbm] * 14,
        out_specs=[vmem, vmem],
        scratch_shapes=[
            pltpu.VMEM((3, atoms), F32),
            pltpu.VMEM(pair_bias_weight.shape, BF16),
            pltpu.VMEM(gains.shape, F32),
            pltpu.VMEM(w_pos.shape, F32),
            pltpu.VMEM(w_pos_out.shape, BF16),
            pltpu.VMEM((atoms_pad, channels), F32),
            pltpu.VMEM((LANES, atoms_pad), F32),
            pltpu.VMEM((atoms_pad, tok_rows), BF16),
            pltpu.VMEM((own, width), F32),
            pltpu.VMEM(pair.shape, BF16),
            pltpu.VMEM((2, tok_rows * half, cols), F32),
            pltpu.VMEM((tok_rows * half, cols), F32),
            pltpu.VMEM(w_atom_token.shape, BF16),
            pltpu.VMEM(w_query_gate.shape, BF16),
            pltpu.VMEM((width, width), BF16),
            pltpu.VMEM((width + w_down.shape[0], width), BF16),
            pltpu.VMEM(w_up.shape, BF16),
            pltpu.VMEM(w_token_atom.shape, BF16),
            pltpu.VMEM((1, atoms_pad), jnp.int32),
            pltpu.VMEM((1, atoms_pad), jnp.int32),
            pltpu.VMEM((n_ba - 1, 1, atoms_pad), jnp.int32),
            pltpu.VMEM((atoms_pad, channels), BF16),
            pltpu.VMEM((atoms_pad, channels), BF16),
            pltpu.VMEM((parts, chips, part_rows, width), BF16),
            pltpu.VMEM((parts, chips - 1, part_rows, width), BF16),
            pltpu.VMEM((parts, part_rows, width), BF16),
            pltpu.VMEM((n_ba, parts, part_rows, width), BF16),
            pltpu.VMEM((2, own, span), BF16),
            pltpu.VMEM((n_ba, own, span), BF16),
            pltpu.VMEM((half, 2 * LANES, keys_n), BF16),
            pltpu.VMEM((span // LANES, tile_heads, keys_n, LANES), BF16),
            pltpu.VMEM((4 * own, half * keys_n), BF16),
            pltpu.VMEM((n_ba, own, span), BF16),
            pltpu.VMEM((n_ba - 1, own, span), BF16),
            pltpu.VMEM((n_ba, 8, LANES), F32),
            pltpu.VMEM((n_ba - 1, 8, LANES), F32),
            pltpu.VMEM((own, w_down.shape[0]), BF16),
            pltpu.VMEM((own, width), BF16),
            pltpu.VMEM((own, channels), BF16),
            pltpu.VMEM((n_ba, own, channels), BF16),
            dma((14,)),
            dma((PAIR_CHUNKS // 2,)),
            dma((2,)),
            dma((2,)),
            dma((2,)),
            dma((1 + parts,)),
            dma((2,)),
            dma((2,)),
            dma((parts,)),
            dma((2,)),
            dma((2,)),
            dma((2,)),
            dma((2,)),
            dma((2 * chips - 1,)),
            dma((2,)),
            dma((2,)),
        ],
        compiler_params=pltpu.CompilerParams(
            collective_id=0, has_side_effects=True, vmem_limit_bytes=48 * 1024 * 1024
        ),
    )(*operands)
    denoised, token_out = pl.pallas_call(
        finish_kernel,
        out_shape=[
            jax.ShapeDtypeStruct((3, atoms), F32),
            jax.ShapeDtypeStruct((tok_rows, width), F32),
        ],
        in_specs=[vmem, vmem],
        out_specs=[vmem, vmem],
        compiler_params=pltpu.CompilerParams(vmem_limit_bytes=8 * 1024 * 1024),
    )(tokens.reshape(tok_rows, width), denoised)
    return denoised, token_out


def solution(mesh):
    in_specs = (
        P(("aa", "ba"), None),
        P(None, ("aa", "ba")),
        P(),
        P(("aa", "ba")),
        P("aa", None),
        P("aa", "ba", None),
    ) + (P(),) * 11
    out_specs = (P(None, ("aa", "ba")), P("aa", None))
    return jax.shard_map(
        functools.partial(on_device, mesh.shape["aa"], mesh.shape["ba"]),
        mesh=mesh,
        in_specs=in_specs,
        out_specs=out_specs,
        check_vma=False,
    )
```

```python
import functools

import jax
import jax.numpy as jnp
from jax import lax
from jax.experimental import pallas as pl
from jax.experimental.pallas import tpu as pltpu
from jax.sharding import PartitionSpec as P

MESH = pl.DeviceIdType.MESH
F32 = jnp.float32
BF16 = jnp.bfloat16
LANES = 128
PAIR_CHUNKS = 8
EARLY_CHUNKS = 3
BIAS_ROWS = 8


def flip(index, mask):
    out = index
    bit = 1
    while bit <= mask:
        if mask & bit:
            out = out + bit - 2 * bit * lax.rem(index // bit, 2)
        bit *= 2
    return out


def far_first(count):
    return sorted(range(1, count), key=lambda m: (-bin(m).count("1"), m))


def norm(values, gain_row):
    mean_value = jnp.mean(values, axis=-1, keepdims=True)
    centered = values - mean_value
    variance = jnp.mean(centered * centered, axis=-1, keepdims=True)
    scaled = centered * lax.rsqrt(variance + 1e-05)
    return scaled if gain_row is None else scaled * gain_row


def dot(a, b):
    return jnp.dot(a, b, preferred_element_type=F32)


def dot_nt(a, b):
    return lax.dot_general(a, b, (((1,), (1,)), ((), ())), preferred_element_type=F32)


def step_kernel(
    n_aa,
    n_ba,
    atom_hbm,
    noisy_hbm,
    noise_ref,
    ids_hbm,
    tok_hbm,
    pair_hbm,
    bias_w_hbm,
    gains_hbm,
    w_pos_hbm,
    wat_hbm,
    wqg_hbm,
    wkv_hbm,
    wo_hbm,
    wup_hbm,
    wdn_hbm,
    wta_hbm,
    w_pos_out_hbm,
    den_ref,
    t_all,
    noisy_ref,
    bias_w_ref,
    gains_ref,
    w_pos_ref,
    w_pos_out_ref,
    v_state,
    v_post,
    v_onehot,
    v_tok,
    v_pair,
    v_bias,
    bias_send,
    v_wat,
    v_wqg,
    v_wkv,
    v_wod,
    v_wup,
    v_wta,
    v_ids,
    ids_mate,
    ids_all,
    state_own,
    state_mate,
    sum_send,
    sum_recv,
    rows_own,
    rows_kv,
    q_own,
    q_all,
    v_km,
    v_vm,
    v_p,
    o_send,
    o_recv,
    st_send,
    st_recv,
    v_inner,
    t_own,
    ta_own,
    ta_all,
    load_sem,
    pair_sem,
    ids_mate_sems,
    ids_sems,
    state_sems,
    sum_sems,
    bias_sems,
    kv_send,
    kv_recv,
    kvm_sems,
    q_sems,
    o_sems,
    st_sems,
    t_sems,
    tm_sems,
    ta_sems,
):
    atoms = noisy_ref.shape[1]
    atoms_pad = v_state.shape[0]
    tok_rows, cols, channels = v_pair.shape
    heads = bias_w_ref.shape[0]
    half = heads // 2
    own, width = v_tok.shape
    head_dim = width // heads
    span = width // 2
    hidden = v_wod.shape[0] - width
    parts, part_rows = rows_own.shape[:2]
    chips = n_ba // 2
    keys_n = 2 * cols
    me_a = lax.axis_index("aa")
    me_b = lax.axis_index("ba")
    core = lax.rem(me_b, 2)
    chip = me_b // 2

    own_start = pl.multiple_of(me_b * own, own)
    span_start = pl.multiple_of(core * span, LANES)
    copies = [
        ("ids", ids_hbm, v_ids.at[0]),
        ("noisy", noisy_hbm, noisy_ref),
        ("atom", atom_hbm, v_state.at[pl.ds(0, atoms)]),
        ("w_pos", w_pos_hbm, w_pos_ref),
        ("wat", wat_hbm, v_wat),
        ("bias_w", bias_w_hbm, bias_w_ref),
        ("gains", gains_hbm, gains_ref),
        ("tok", tok_hbm.at[pl.ds(own_start, own)], v_tok),
        ("w_pos_out", w_pos_out_hbm, w_pos_out_ref),
        ("wqg", wqg_hbm, v_wqg),
        ("wkv", wkv_hbm.at[:, pl.ds(span_start, span)], v_wkv.at[:, pl.ds(0, span)]),
        (
            "wkv",
            wkv_hbm.at[:, pl.ds(pl.multiple_of(width + core * span, LANES), span)],
            v_wkv.at[:, pl.ds(span, span)],
        ),
        ("wod", wo_hbm, v_wod.at[pl.ds(0, width)]),
        ("wup", wup_hbm, v_wup),
        ("wod", wdn_hbm, v_wod.at[pl.ds(width, hidden)]),
        ("wta", wta_hbm, v_wta),
    ]
    names = list(dict.fromkeys(name for name, _, _ in copies))

    def load(name):
        for key, src, dst in copies:
            if key == name:
                pltpu.make_async_copy(src, dst, load_sem.at[names.index(name)]).start()

    def take(whole, sem):
        pltpu.make_async_copy(whole, whole, sem).wait()

    def loaded(name, whole):
        take(whole, load_sem.at[names.index(name)])

    step = tok_rows // PAIR_CHUNKS
    pair_loads = [
        pltpu.make_async_copy(
            pair_hbm.at[pl.ds(c * step, 2 * step)],
            v_pair.at[pl.ds(c * step, 2 * step)],
            pair_sem.at[c // 2],
        )
        for c in range(0, PAIR_CHUNKS, 2)
    ]
    for name in names[:5]:
        load(name)

    def at(a, b):
        return {"aa": a, "ba": b}

    def greet(device):
        pl.semaphore_signal(barrier, inc=1, device_id=device, device_id_type=MESH)

    barrier = pltpu.get_barrier_semaphore()
    for x in range(1, n_ba):
        greet(at(me_a, flip(me_b, x)))
    block = me_b // chips
    column = 2 * me_a + block
    for x in range(1, n_aa):
        greet(at(flip(me_a, x), column))

    @pl.when(chip != me_a)
    def _():
        for j in range(chips):
            greet(at(chip, core * chips + j))

    greetings = n_ba - 1 + n_aa - 1 + jnp.where(chip != me_a, chips, 0)

    for name in names[5:8]:
        load(name)
    for copy in pair_loads:
        copy.start()
    for name in names[8:]:
        load(name)
    if atoms_pad > atoms:
        v_state[pl.ds(atoms, atoms_pad - atoms), :] = jnp.zeros(
            (atoms_pad - atoms, channels), F32
        )

    def ba_copy(src, dst, sems, x, slot=1):
        return pltpu.make_async_remote_copy(
            src_ref=src,
            dst_ref=dst,
            send_sem=sems.at[0],
            recv_sem=sems.at[slot],
            device_id=at(me_a, flip(me_b, x)),
            device_id_type=MESH,
        )

    order = far_first(n_ba)
    chip_order = far_first(chips)

    loaded("noisy", noisy_ref)
    sigma = jnp.full((3, atoms), noise_ref[0], F32)
    inv_scale = 1.0 / jnp.sqrt(sigma * sigma + 1.0)
    v_post[...] = jnp.full(v_post.shape, -1.0, F32)
    v_post[0:3, 0:atoms] = noisy_ref[...] * inv_scale
    loaded("ids", v_ids.at[0])
    ids_row = v_ids[...]
    v_post[3:4, :] = ids_row.astype(F32)
    columns = v_post[...].T
    loaded("w_pos", w_pos_ref)
    loaded("atom", v_state.at[pl.ds(0, atoms)])
    state = v_state[...]
    for c in range(3):
        state = state + columns[:, c : c + 1] * w_pos_ref[c : c + 1, :]
    v_state[...] = state
    rounded = state.astype(BF16)
    state_own[...] = rounded

    pl.semaphore_wait(barrier, greetings)
    ba_copy(state_own, state_mate, state_sems, 1).start()
    ba_copy(v_ids, ids_mate, ids_mate_sems, 1).start()
    for x in order:
        ba_copy(v_ids, ids_all.at[x - 1], ids_sems, x).start()
    group = max(1, parts // 2)

    def select(ids, first):
        row = lax.broadcasted_iota(jnp.int32, (group * chips * part_rows, atoms_pad), 0)
        token = lax.rem(row, part_rows) + 2 * own * lax.rem(row // part_rows, chips)
        token = token + part_rows * (first + row // (part_rows * chips))
        token = token + (own * core + me_a * tok_rows)
        return jnp.where(token == ids, 1.0, 0.0).astype(BF16)

    loaded("wat", v_wat)
    hidden_own = jnp.maximum(dot(rounded, v_wat[...]), 0.0).astype(BF16)
    firsts = range(0, parts, group)
    own_sums = [dot(select(ids_row, first), hidden_own) for first in firsts]
    take(ids_mate, ids_mate_sems.at[1])
    selectors = [select(ids_mate[...], first) for first in firsts]
    take(state_mate, state_sems.at[1])
    hidden_mate = jnp.maximum(dot(state_mate[...], v_wat[...]), 0.0).astype(BF16)
    for first, sums, selector in zip(firsts, own_sums, selectors):
        chip_sums = sums + dot(selector, hidden_mate)
        sum_send[first : first + group] = chip_sums.astype(BF16).reshape(
            group, chips, part_rows, width
        )
        for part in range(first, first + group):
            for d in chip_order:
                ba_copy(
                    sum_send.at[part, flip(chip, d)],
                    sum_recv.at[part, d - 1],
                    sum_sems,
                    2 * d,
                    1 + part,
                ).start()

    lane_id = lax.broadcasted_iota(jnp.int32, (atoms_pad, tok_rows), 1) + me_a * tok_rows
    v_onehot[...] = jnp.where(columns[:, 3:4] == lane_id.astype(F32), 1.0, 0.0).astype(BF16)
    loaded("bias_w", bias_w_ref)
    weights_all = bias_w_ref[...].astype(F32)
    first_half, second_half = weights_all[0:half], weights_all[half:heads]
    bias_w = jnp.concatenate(
        [
            jnp.where(core == 0, first_half, second_half),
            jnp.where(core == 0, second_half, first_half),
        ],
        axis=0,
    ).astype(BF16)
    bias_rows = step * half
    bias_copies = [
        ba_copy(
            bias_send.at[pl.ds(c * bias_rows, bias_rows)],
            v_bias.at[core, pl.ds(c * bias_rows, bias_rows)],
            bias_sems,
            1,
        )
        for c in range(PAIR_CHUNKS)
    ]

    def bias_chunk(c):
        if c % 2 == 0:
            pair_loads[c // 2].wait()

        def rows(r, carry):
            start = c * step + r * BIAS_ROWS
            block = v_pair[pl.ds(start, BIAS_ROWS)].reshape(BIAS_ROWS * cols, channels)
            out = dot_nt(bias_w, block)
            for i in range(BIAS_ROWS):
                where = pl.ds(pl.multiple_of((start + i) * half, half), half)
                v_bias[core, where, :] = out[0:half, i * cols : (i + 1) * cols]
                bias_send[where, :] = out[half:heads, i * cols : (i + 1) * cols]
            return carry

        lax.fori_loop(0, step // BIAS_ROWS, rows, 0)
        bias_copies[c].start()

    for c in range(EARLY_CHUNKS):
        bias_chunk(c)

    own_row = lax.broadcasted_iota(jnp.int32, (own, atoms_pad), 0) + (
        me_a * tok_rows + me_b * own
    )
    take(ids_all, ids_sems.at[1])
    hits = jnp.where(own_row == ids_row, 1.0, 0.0)
    for x in order:
        hits = hits + jnp.where(own_row == ids_all[x - 1], 1.0, 0.0)
    counts = jnp.sum(hits, axis=1, keepdims=True)
    loaded("tok", v_tok)
    loaded("gains", gains_ref)

    low = jnp.where(2 * me_a < n_aa, me_a, n_aa - 1 - me_a)

    def plane(k):
        if k < 0:
            return me_a
        place = n_aa - 1 - k
        place = jnp.where(place > low, place, k - (n_aa - 1 - low))
        return jnp.where(2 * me_a < n_aa, place, n_aa - 1 - place)

    def kv_copy(k, part):
        return pltpu.make_async_remote_copy(
            src_ref=rows_own.at[part],
            dst_ref=rows_kv.at[me_b, part],
            send_sem=kv_send.at[1 if k >= 0 else 0],
            recv_sem=kv_recv.at[part],
            device_id=at(plane(k), column),
            device_id_type=MESH,
        )

    for part in range(parts):
        rows = pl.ds(part * part_rows, part_rows)
        summed = sum_send[part, chip].astype(F32)
        take(sum_recv.at[part], sum_sems.at[1 + part])
        for d in chip_order:
            summed = summed + sum_recv[part, d - 1].astype(F32)
        tokens_start = (
            v_tok[rows, :] + summed / counts[part * part_rows : (part + 1) * part_rows]
        )
        v_tok[rows, :] = tokens_start
        rows_own[part] = norm(tokens_start, gains_ref[0:1, :]).astype(BF16)
        for k in range(n_aa - 1):
            kv_copy(k, part).start()

        @pl.when(column != me_b)
        def _():
            kv_copy(-1, part).start()

        @pl.when(column == me_b)
        def _():
            pltpu.make_async_copy(
                rows_own.at[part], rows_kv.at[me_b, part], kv_recv.at[part]
            ).start()

    normed = rows_own[...].reshape(own, width)
    loaded("wqg", v_wqg)
    query = dot(normed, v_wqg[:, 0:width]).astype(BF16)
    for c in range(2):
        q_own[c] = query[:, c * span : (c + 1) * span]
    q_all[me_b] = q_own[core]
    gate = jax.nn.sigmoid(dot(normed, v_wqg[:, width : 2 * width])).astype(BF16)

    for c in range(EARLY_CHUNKS, PAIR_CHUNKS):
        bias_chunk(c)
        if c == EARLY_CHUNKS + 1:
            for x in order:
                ba_copy(q_own.at[lax.rem(core + x, 2)], q_all.at[me_b], q_sems, x).start()
    for part in range(parts):
        rows = rows_kv.at[pl.ds(core * chips, chips), part]
        take(rows, kv_recv.at[part])
        ba_copy(rows, rows, kvm_sems, 1).start()
    loaded("wkv", v_wkv)
    chip_pieces = rows_kv.at[pl.ds(0, chips)]
    spans = []
    for h in range(half):
        lo = h * head_dim // LANES * LANES
        hi = ((h + 1) * head_dim + LANES - 1) // LANES * LANES
        spans.append((lo, hi))
    tiles = []
    for t in range(span // LANES):
        tiles.append((t * LANES // head_dim, (t * LANES + LANES - 1) // head_dim))

    def project(which):
        pieces = rows_kv[pl.ds(which * chips, chips)].reshape(cols, width)
        key_value = dot(pieces, v_wkv[...])
        keys = pl.ds(pl.multiple_of(which * cols, cols), cols)
        turned = [
            key_value[:, t * LANES : (t + 1) * LANES].T for t in range(span // LANES)
        ]
        for h, (lo, hi) in enumerate(spans):
            for t in range(lo // LANES, hi // LANES):
                row = lax.broadcasted_iota(jnp.int32, (LANES, cols), 0) + t * LANES
                mine = (row >= h * head_dim) & (row < (h + 1) * head_dim)
                v_km[h, t * LANES - lo : (t + 1) * LANES - lo, keys] = jnp.where(
                    mine, turned[t], 0.0
                ).astype(BF16)
        for t, (h0, h1) in enumerate(tiles):
            piece = key_value[:, span + t * LANES : span + (t + 1) * LANES]
            lane = lax.broadcasted_iota(jnp.int32, (cols, LANES), 1) + t * LANES
            for h in range(h0, h1 + 1):
                mine = (lane >= h * head_dim) & (lane < (h + 1) * head_dim)
                v_vm[t, h - h0, keys, :] = jnp.where(mine, piece, 0.0).astype(BF16)

    project(core)
    take(chip_pieces, kvm_sems.at[1])
    project(1 - core)

    q_pieces = q_all.at[pl.ds(0, n_ba - 1)]
    take(q_pieces, q_sems.at[1])
    take(bias_send, bias_sems.at[1])

    scale = head_dim ** (-0.5)
    rows2 = 2 * own
    batches = [chip_order[:1]] + [chip_order[n : n + 2] for n in range(1, chips - 1, 2)] + [[0]]
    groups = own // 8
    for duos in batches:
        places = [flip(chip, d) for d in duos]
        many = len(places)
        lane = lax.broadcasted_iota(jnp.int32, (many * rows2, LANES), 1)
        top_lane = lane - half * core
        stats = jnp.zeros((many * rows2, LANES), F32)
        q_rows = jnp.concatenate(
            [q_all[pl.ds(2 * duo, 2)].reshape(rows2, span) for duo in places], axis=0
        )
        for h in range(half):
            lo, hi = spans[h]
            scores = dot(q_rows[:, lo:hi], v_km[h, 0 : hi - lo, :]) * scale
            pair_bias = [
                jnp.concatenate(
                    [
                        v_bias[k, pl.ds(duo * (rows2 * half) + h, rows2, stride=half), :]
                        for duo in places
                    ],
                    axis=0,
                )
                for k in range(2)
            ]
            both = [scores[:, k * cols : (k + 1) * cols] + pair_bias[k] for k in range(2)]
            top = jnp.max(jnp.maximum(both[0], both[1]), axis=1, keepdims=True)
            both = [jnp.exp(one - top) for one in both]
            total = jnp.sum(both[0] + both[1], axis=1, keepdims=True)
            stats = jnp.where(top_lane == h, top, stats)
            stats = jnp.where(top_lane == heads + h, total, stats)
            for k in range(2):
                v_p[0 : many * rows2, h * keys_n + k * cols : h * keys_n + (k + 1) * cols] = both[k].astype(BF16)
        for t, (h0, h1) in enumerate(tiles):
            count = (h1 - h0 + 1) * keys_n
            out = dot(
                v_p[0 : many * rows2, h0 * keys_n : h0 * keys_n + count],
                v_vm[t, 0 : h1 - h0 + 1].reshape(count, LANES),
            ).astype(BF16)
            for i, duo in enumerate(places):
                o_send[pl.ds(2 * duo, 2), :, t * LANES : (t + 1) * LANES] = out[
                    i * rows2 : (i + 1) * rows2
                ].reshape(2, own, LANES)
        for i, duo in enumerate(places):
            for c in range(2):
                at_row = i * rows2 + c * own
                packed = stats[at_row : at_row + 8]
                for g in range(1, groups):
                    piece = stats[at_row + 8 * g : at_row + 8 * g + 8]
                    piece = pltpu.roll(piece, 2 * heads * g, 1)
                    packed = jnp.where(lane[0:8] >= 2 * heads * g, piece, packed)
                st_send[2 * duo + c] = packed
        for d in duos:
            for x in (2 * d + 1, 2 * d):
                if x:
                    target = flip(me_b, x)
                    ba_copy(st_send.at[target], st_recv.at[x - 1], st_sems, x).start()
                    ba_copy(o_send.at[target], o_recv.at[x - 1], o_sems, x).start()

    lane = lax.broadcasted_iota(jnp.int32, (own, LANES), 1)

    def unpack(packed):
        parts = [packed]
        for g in range(1, groups):
            parts.append(pltpu.roll(packed, LANES - 2 * heads * g, 1))
        return jnp.concatenate(parts, axis=0)

    take(st_recv, st_sems.at[1])
    tops = []
    for d in range(chips):
        mine = st_recv[2 * d - 1] if d else st_send[me_b]
        tops.append(unpack(mine + st_recv[2 * d]))
    overall = tops[0]
    for top in tops[1:]:
        overall = jnp.maximum(overall, top)
    factors = [jnp.exp(top - overall) for top in tops]
    denominator = jnp.zeros((own, LANES), F32)
    for factor, top in zip(factors, tops):
        denominator = denominator + factor * pltpu.roll(top, LANES - heads, 1)
    head_row = lax.broadcasted_iota(jnp.int32, (LANES, width), 0)
    head_lane = lax.broadcasted_iota(jnp.int32, (LANES, width), 1)
    inside = (head_lane >= head_row * head_dim) & (head_lane < (head_row + 1) * head_dim)
    spread = jnp.where(inside, 1.0, 0.0).astype(BF16)
    live = lane < heads
    shares = jnp.concatenate(
        [jnp.where(live, factor / denominator, 0.0) for factor in factors], axis=0
    )
    coarse = shares.astype(BF16)
    fine = (shares - coarse.astype(F32)).astype(BF16)
    wide = dot(coarse, spread) + dot(fine, spread)
    take(o_recv, o_sems.at[1])
    left = jnp.zeros((own, span), F32)
    right = jnp.zeros((own, span), F32)
    for d in range(chips):
        mine = (o_recv[2 * d - 1] if d else o_send[me_b]).astype(F32)
        other = o_recv[2 * d].astype(F32)
        part = wide[d * own : (d + 1) * own]
        left = left + part[:, 0:span] * jnp.where(core == 0, mine, other)
        right = right + part[:, span:width] * jnp.where(core == 0, other, mine)
    attended = jnp.concatenate([left, right], axis=1)
    mixed = (attended * gate.astype(F32)).astype(BF16)
    loaded("wod", v_wod)
    tokens_mid = v_tok[...] + dot(mixed, v_wod[0:width, :])
    normed_mid = norm(tokens_mid, gains_ref[1:2, :]).astype(BF16)
    loaded("wup", v_wup)
    part = 512
    for n in range(0, hidden, part):
        first = dot(normed_mid, v_wup[:, n : n + part])
        second = dot(normed_mid, v_wup[:, hidden + n : hidden + n + part])
        v_inner[:, n : n + part] = (first * jax.nn.sigmoid(first) * second).astype(BF16)
    outs = []

    def share(c):
        columns_c = pl.ds(c * span, span)
        for d in chip_order:
            ba_copy(
                t_own.at[:, columns_c],
                t_all.at[me_b, :, columns_c],
                t_sems,
                2 * d,
                c * (chips - 1) + d,
            ).start()

    for c in range(2):
        out = dot(v_inner[...], v_wod[width : width + hidden, c * span : (c + 1) * span])
        out = tokens_mid[:, c * span : (c + 1) * span] + out
        outs.append(out)
        t_own[:, c * span : (c + 1) * span] = out.astype(BF16)
        t_all[me_b, :, c * span : (c + 1) * span] = out.astype(BF16)
        if c == 0:
            share(0)
    token_out = jnp.concatenate(outs, axis=1)
    loaded("wta", v_wta)
    normed_out = norm(token_out, gains_ref[2:3, :]).astype(BF16)
    token_atom = dot(normed_out, v_wta[...]).astype(BF16)
    ta_own[...] = token_atom
    ta_all[me_b] = token_atom
    for x in order:
        ba_copy(ta_own, ta_all.at[me_b], ta_sems, x).start()
    share(1)
    ba_copy(t_own, t_all.at[me_b], tm_sems, 1).start()
    loaded("w_pos_out", w_pos_out_ref)
    for c in range(2):
        for d in range(1, chips):
            rows = t_all.at[flip(me_b, 2 * d), :, pl.ds(c * span, span)]
            take(rows, t_sems.at[c * (chips - 1) + d])
            ba_copy(rows, rows, tm_sems, 1).start()
    ta_pieces = ta_all.at[pl.ds(0, n_ba - 1)]
    take(ta_pieces, ta_sems.at[1])
    picked = dot(v_onehot[...], ta_all[...].reshape(tok_rows, channels))
    atom_normed = norm(v_state[...] + picked, None).astype(BF16)
    update = dot_nt(w_pos_out_ref[...], atom_normed)[:, 0:atoms]
    den_ref[...] = noisy_ref[...] * (inv_scale * inv_scale) + update * (sigma * inv_scale)
    t_pieces = t_all.at[pl.ds(0, chips)]
    take(t_pieces, tm_sems.at[1])
    for whole, sem in (
        (state_mate, state_sems),
        (ids_mate, ids_mate_sems),
        (ids_all, ids_sems),
        (sum_recv, sum_sems),
        (bias_send, bias_sems),
        (chip_pieces, kvm_sems),
        (q_pieces, q_sems),
        (st_recv, st_sems),
        (o_recv, o_sems),
        (t_all.at[pl.ds(0, chips - 1)], t_sems),
        (t_pieces, tm_sems),
        (ta_pieces, ta_sems),
    ):
        take(whole, sem.at[0])
    take(rows_kv.at[pl.ds(0, n_aa - 1)], kv_send.at[1])

    @pl.when(column != me_b)
    def _():
        take(rows_own, kv_send.at[0])


def finish_kernel(tok_ref, den_ref, den_out_ref, tok_out_ref):
    den_out_ref[...] = den_ref[...]
    tok_out_ref[...] = tok_ref[...].astype(F32)


def on_device(
    n_aa,
    n_ba,
    atom_cond,
    noisy_pos,
    noise_level,
    atom_token,
    token_cond,
    pair,
    pair_bias_weight,
    gains,
    w_pos,
    w_atom_token,
    w_query_gate,
    w_key_value,
    w_attn_out,
    w_up,
    w_down,
    w_token_atom,
    w_pos_out,
):
    atoms, channels = atom_cond.shape
    atoms_pad = -(-atoms // LANES) * LANES
    tok_rows, width = token_cond.shape
    cols = pair.shape[1]
    heads = pair_bias_weight.shape[0]
    own = tok_rows // n_ba
    chips = n_ba // 2
    half, span, keys_n = heads // 2, width // 2, 2 * cols
    part_rows = 8
    parts = own // part_rows
    head_dim = width // heads
    if tok_rows != 2 * cols or chips != n_aa:
        raise ValueError("unsupported mesh")
    tile_heads = max(
        (t * LANES + LANES - 1) // head_dim - t * LANES // head_dim + 1
        for t in range(span // LANES)
    )
    ids = atom_token
    if atoms_pad > atoms:
        ids = jnp.pad(atom_token, (0, atoms_pad - atoms), constant_values=-1)
    vmem = pl.BlockSpec(memory_space=pltpu.VMEM)
    smem = pl.BlockSpec(memory_space=pltpu.SMEM)
    hbm = pl.BlockSpec(memory_space=pltpu.HBM)
    dma = pltpu.SemaphoreType.DMA
    operands = [
        pltpu.with_memory_space_constraint(value, pltpu.HBM) if value.size > 1 else value
        for value in (
            atom_cond,
            noisy_pos,
            noise_level,
            ids,
            token_cond,
            pair,
            pair_bias_weight,
            gains,
            w_pos,
            w_atom_token,
            w_query_gate,
            w_key_value,
            w_attn_out,
            w_up,
            w_down,
            w_token_atom,
            w_pos_out,
        )
    ]
    denoised, tokens = pl.pallas_call(
        functools.partial(step_kernel, n_aa, n_ba),
        out_shape=[
            jax.ShapeDtypeStruct((3, atoms), F32),
            jax.ShapeDtypeStruct((n_ba, own, width), BF16),
        ],
        in_specs=[hbm, hbm, smem] + [hbm] * 14,
        out_specs=[vmem, vmem],
        scratch_shapes=[
            pltpu.VMEM((3, atoms), F32),
            pltpu.VMEM(pair_bias_weight.shape, BF16),
            pltpu.VMEM(gains.shape, F32),
            pltpu.VMEM(w_pos.shape, F32),
            pltpu.VMEM(w_pos_out.shape, BF16),
            pltpu.VMEM((atoms_pad, channels), F32),
            pltpu.VMEM((LANES, atoms_pad), F32),
            pltpu.VMEM((atoms_pad, tok_rows), BF16),
            pltpu.VMEM((own, width), F32),
            pltpu.VMEM(pair.shape, BF16),
            pltpu.VMEM((2, tok_rows * half, cols), F32),
            pltpu.VMEM((tok_rows * half, cols), F32),
            pltpu.VMEM(w_atom_token.shape, BF16),
            pltpu.VMEM(w_query_gate.shape, BF16),
            pltpu.VMEM((width, width), BF16),
            pltpu.VMEM((width + w_down.shape[0], width), BF16),
            pltpu.VMEM(w_up.shape, BF16),
            pltpu.VMEM(w_token_atom.shape, BF16),
            pltpu.VMEM((1, atoms_pad), jnp.int32),
            pltpu.VMEM((1, atoms_pad), jnp.int32),
            pltpu.VMEM((n_ba - 1, 1, atoms_pad), jnp.int32),
            pltpu.VMEM((atoms_pad, channels), BF16),
            pltpu.VMEM((atoms_pad, channels), BF16),
            pltpu.VMEM((parts, chips, part_rows, width), BF16),
            pltpu.VMEM((parts, chips - 1, part_rows, width), BF16),
            pltpu.VMEM((parts, part_rows, width), BF16),
            pltpu.VMEM((n_ba, parts, part_rows, width), BF16),
            pltpu.VMEM((2, own, span), BF16),
            pltpu.VMEM((n_ba, own, span), BF16),
            pltpu.VMEM((half, 2 * LANES, keys_n), BF16),
            pltpu.VMEM((span // LANES, tile_heads, keys_n, LANES), BF16),
            pltpu.VMEM((4 * own, half * keys_n), BF16),
            pltpu.VMEM((n_ba, own, span), BF16),
            pltpu.VMEM((n_ba - 1, own, span), BF16),
            pltpu.VMEM((n_ba, 8, LANES), F32),
            pltpu.VMEM((n_ba - 1, 8, LANES), F32),
            pltpu.VMEM((own, w_down.shape[0]), BF16),
            pltpu.VMEM((own, width), BF16),
            pltpu.VMEM((own, channels), BF16),
            pltpu.VMEM((n_ba, own, channels), BF16),
            dma((14,)),
            dma((PAIR_CHUNKS // 2,)),
            dma((2,)),
            dma((2,)),
            dma((2,)),
            dma((1 + parts,)),
            dma((2,)),
            dma((2,)),
            dma((parts,)),
            dma((2,)),
            dma((2,)),
            dma((2,)),
            dma((2,)),
            dma((2 * chips - 1,)),
            dma((2,)),
            dma((2,)),
        ],
        compiler_params=pltpu.CompilerParams(
            collective_id=0, has_side_effects=True, vmem_limit_bytes=48 * 1024 * 1024
        ),
    )(*operands)
    denoised, token_out = pl.pallas_call(
        finish_kernel,
        out_shape=[
            jax.ShapeDtypeStruct((3, atoms), F32),
            jax.ShapeDtypeStruct((tok_rows, width), F32),
        ],
        in_specs=[vmem, vmem],
        out_specs=[vmem, vmem],
        compiler_params=pltpu.CompilerParams(vmem_limit_bytes=8 * 1024 * 1024),
    )(tokens.reshape(tok_rows, width), denoised)
    return denoised, token_out


def solution(mesh):
    in_specs = (
        P(("aa", "ba"), None),
        P(None, ("aa", "ba")),
        P(),
        P(("aa", "ba")),
        P("aa", None),
        P("aa", "ba", None),
    ) + (P(),) * 11
    out_specs = (P(None, ("aa", "ba")), P("aa", None))
    return jax.shard_map(
        functools.partial(on_device, mesh.shape["aa"], mesh.shape["ba"]),
        mesh=mesh,
        in_specs=in_specs,
        out_specs=out_specs,
        check_vma=False,
    )
```
